32 devices in a mesh: gx: 4 (over y, core), gy: 8 (over z, x).
Axes of the slice: x: 2, y: 2, z: 4, core: 2. Of those that a mesh axis runs over, the one named last changes fastest.
Arguments:
- local_schur: float32 [4096, 8192], P('gx', 'gy'), as said below
- boundary_map: int32 [4, 8, 1024], P('gx', 'gy'), may hold values from 0 to 1023, each once within a row
- order_first: int32 [2, 8, 256], P(None, 'gy'), may hold values from 0 to 255, each once within a row
- order_second: int32 [2, 4, 512], replicated, may hold values from 0 to 511, each once within a row
Outputs:
- first_factor: float32 [512, 2048], P('gx', 'gy')
- first_panel: float32 [3072, 2048], P('gx', 'gy')
- second_factor: float32 [1024, 2048], P('gx', 'gy')
- second_panel: float32 [2048, 4096], P('gx', 'gy')
- merged_schur: float32 [2048, 16384], P('gx', 'gy')
The draws below stay inside these ranges and needn't reach their ends.
Inputs may be any that keep to these rules, and one draw needn't show every extreme that they name: `local_schur`: each 1024 x 1024 block is symmetric positive definite. `boundary_map`: the 1024 slots of a subdomain hold each of its boundary nodes once. `order_first`: each row lists the 256 nodes of one separator once each. `order_second`: each row lists the 512 nodes of one separator once each.
All inputs are finite; a program needn't handle non-finite values.
Results may differ from the reference program's by a relative error of at most 0.0001.
Values sent between devices are 32-bit elements; how exact they have to be, the bound alone decides.
A program may use at most 128 MiB of HBM per device.

```python
import jax
import jax.numpy as jnp
from jax import lax

SEP = 256
BND = 1024
SUB_ROWS = 4
SUB_COLS = 8
PAIR_ROWS = 2
PAIR_COLS = 4
ROWS_ALL = 4096
COLS_ALL = 8192


def draw_local_schur(key, part):
    sub_rows = ROWS_ALL // BND
    sub_cols = COLS_ALL // BND
    key_list = jax.random.split(jax.random.fold_in(key, 17), 3)
    grid_shape = (sub_rows, BND, sub_cols, BND)
    node_shape = (sub_rows, BND, sub_cols)
    noise_part = jax.random.uniform(key_list[0], grid_shape, jnp.float32, -1.0, 1.0)
    noise_part = 0.5 * (noise_part + jnp.transpose(noise_part, (0, 3, 2, 1)))
    spread = jax.random.uniform(key_list[1], node_shape, jnp.float32, 0.6, 1.4)
    margin = jax.random.uniform(key_list[2], node_shape, jnp.float32, 0.05, 1.0)
    row_scale = spread[:, :, :, None]
    col_scale = jnp.transpose(spread, (0, 2, 1))[:, None, :, :]
    slot_index = jnp.arange(BND, dtype=jnp.int32)
    product = (slot_index[:, None] + 1) * (slot_index[None, :] + 1) % (2 * (BND + 1))
    sine_table = jnp.sqrt(2.0 / (BND + 1.0)) * jnp.sin(jnp.pi * product.astype(jnp.float32) / (BND + 1.0))
    diagonal = (slot_index[:, None] == slot_index[None, :])[None, :, None, :]
    noise_scale = 0.3 / jnp.sqrt(jnp.float32(BND))
    matrix = 1.5 * row_scale * sine_table[None, :, None, :] * col_scale
    matrix = matrix + jnp.where(diagonal, 0.0, noise_scale * noise_part)
    matrix = matrix + jnp.where(diagonal, 3.3 * (1.0 + margin[:, :, :, None]), 0.0)
    return matrix.reshape(ROWS_ALL, COLS_ALL).astype(jnp.float32)


def setup_inputs(seed: int = 0) -> dict:
    seeds = jax.random.split(jax.random.key(seed), 5)
    return {
        "local_schur": draw_local_schur(jax.random.fold_in(seeds[4], 71), 0),
        "boundary_map": jax.vmap(lambda own: jax.random.permutation(own, BND))(jax.random.split(seeds[1], SUB_ROWS * SUB_COLS)).reshape((SUB_ROWS, SUB_COLS, BND)).astype(jnp.int32),
        "order_first": jax.vmap(lambda own: jax.random.permutation(own, SEP))(jax.random.split(seeds[2], PAIR_ROWS * SUB_COLS)).reshape((PAIR_ROWS, SUB_COLS, SEP)).astype(jnp.int32),
        "order_second": jax.vmap(lambda own: jax.random.permutation(own, 2 * SEP))(jax.random.split(seeds[3], PAIR_ROWS * PAIR_COLS)).reshape((PAIR_ROWS, PAIR_COLS, 2 * SEP)).astype(jnp.int32),
    }


highest = lax.Precision.HIGHEST

def reorder(sub_block, slots, left_side, upper_side):
    edge_index = slots // SEP
    west_pos = jnp.where(left_side, 1, 0).astype(jnp.int32)
    north_pos = jnp.where(upper_side, 2, 3).astype(jnp.int32)
    new_edge = jnp.where(edge_index == 0, west_pos, jnp.where(edge_index == 1, 1 - west_pos, jnp.where(edge_index == 2, north_pos, 5 - north_pos)))
    target = (new_edge * SEP + slots % SEP).astype(jnp.int32)
    inverse = jnp.zeros_like(target).at[target].set(jnp.arange(target.shape[0], dtype=jnp.int32))
    return sub_block[inverse][:, inverse]

def gram_rows(left_rows, right_rows):
    return jnp.einsum('ik,jk->ij', left_rows.astype(jnp.float32), right_rows.astype(jnp.float32), precision=highest, preferred_element_type=jnp.float32)

def panel_solve(factor, coupling):
    return lax.linalg.triangular_solve(factor, coupling, left_side=False, lower=True, transpose_a=True)

def pick_blocks(matrix, row_list, col_list):
    rows_built = []
    for row_block in row_list:
        pieces = [matrix[row_block * SEP:(row_block + 1) * SEP, col_block * SEP:(col_block + 1) * SEP] for col_block in col_list]
        rows_built.append(jnp.concatenate(pieces, axis=1))
    return jnp.concatenate(rows_built, axis=0)

def block_diagonal(upper_part, lower_part):
    zero_part = jnp.zeros_like(upper_part)
    return jnp.concatenate([jnp.concatenate([upper_part, zero_part], axis=1), jnp.concatenate([zero_part, lower_part], axis=1)], axis=0)

def first_level(upper_block, lower_block, order_one):
    inner_rows = 3 * SEP
    pivot_one = upper_block[inner_rows:, inner_rows:] + lower_block[inner_rows:, inner_rows:]
    factor_one = jnp.linalg.cholesky(pivot_one[order_one][:, order_one])
    coupling = jnp.concatenate([upper_block[:inner_rows, inner_rows:], lower_block[:inner_rows, inner_rows:]], axis=0)[:, order_one]
    panels = panel_solve(factor_one, coupling)
    placed = block_diagonal(upper_block[:inner_rows, :inner_rows], lower_block[:inner_rows, :inner_rows])
    reduced = placed - gram_rows(panels, panels)
    return (factor_one, panels, reduced)

def reference(local_schur, boundary_map, order_first, order_second):
    outputs_init = (jnp.zeros((PAIR_ROWS * SEP, SUB_COLS * SEP), jnp.float32), jnp.zeros((SUB_ROWS * 3 * SEP, SUB_COLS * SEP), jnp.float32), jnp.zeros((SUB_ROWS * SEP, SUB_COLS * SEP), jnp.float32), jnp.zeros((SUB_ROWS * 2 * SEP, SUB_COLS * 2 * SEP), jnp.float32), jnp.zeros((SUB_ROWS * 2 * SEP, SUB_COLS * 8 * SEP), jnp.float32))
    half_rows = SEP // 2

    def one_group(group_index, outputs_now):
        group_index = jnp.asarray(group_index).astype(jnp.int32)
        pair_row = (group_index // PAIR_COLS).astype(jnp.int32)
        pair_col = (group_index % PAIR_COLS).astype(jnp.int32)
        zero_index = (pair_row * 0).astype(jnp.int32)
        order_two = lax.dynamic_slice(order_second, (pair_row, pair_col, zero_index), (1, 1, 2 * SEP))[0, 0]
        first_factor, first_panel, second_factor, second_panel, merged_schur = outputs_now
        reduced_sides = []
        for col_side in range(2):
            block_col = (pair_col + col_side * PAIR_COLS).astype(jnp.int32)
            ordered = []
            for row_side in range(2):
                block_row = (pair_row + row_side * PAIR_ROWS).astype(jnp.int32)
                sub_block = lax.dynamic_slice(local_schur, (block_row * BND, block_col * BND), (BND, BND))
                slots = lax.dynamic_slice(boundary_map, (block_row, block_col, zero_index), (1, 1, BND))[0, 0]
                ordered.append(reorder(sub_block, slots, col_side == 0, row_side == 0))
            order_one = lax.dynamic_slice(order_first, (pair_row, block_col, zero_index), (1, 1, SEP))[0, 0]
            factor_one, panels, reduced = first_level(ordered[0], ordered[1], order_one)
            column = (block_col * SEP).astype(jnp.int32)
            first_factor = lax.dynamic_update_slice(first_factor, factor_one[:half_rows], (pair_row * half_rows, column))
            first_factor = lax.dynamic_update_slice(first_factor, factor_one[half_rows:], ((pair_row + PAIR_ROWS) * half_rows, column))
            first_panel = lax.dynamic_update_slice(first_panel, panels[:3 * SEP], (pair_row * (3 * SEP), column))
            first_panel = lax.dynamic_update_slice(first_panel, panels[3 * SEP:], ((pair_row + PAIR_ROWS) * (3 * SEP), column))
            reduced_sides.append(reduced)
        left_reduced, right_reduced = reduced_sides
        inner_set = [0, 3]
        outer_set = [1, 2, 4, 5]
        pivot_two = pick_blocks(left_reduced, inner_set, inner_set) + pick_blocks(right_reduced, inner_set, inner_set)
        factor_two = jnp.linalg.cholesky(pivot_two[order_two][:, order_two])
        coupling_two = jnp.concatenate([pick_blocks(left_reduced, outer_set, inner_set), pick_blocks(right_reduced, outer_set, inner_set)], axis=0)[:, order_two]
        panels_two = panel_solve(factor_two, coupling_two)
        placed_two = block_diagonal(pick_blocks(left_reduced, outer_set, outer_set), pick_blocks(right_reduced, outer_set, outer_set))
        merged = placed_two - gram_rows(panels_two, panels_two)
        for row_side in range(2):
            for col_side in range(2):
                block_row = (pair_row + row_side * PAIR_ROWS).astype(jnp.int32)
                block_col = (pair_col + col_side * PAIR_COLS).astype(jnp.int32)
                slot = 2 * col_side + row_side
                second_factor = lax.dynamic_update_slice(second_factor, factor_two[row_side * SEP:(row_side + 1) * SEP, col_side * SEP:(col_side + 1) * SEP], (block_row * SEP, block_col * SEP))
                second_panel = lax.dynamic_update_slice(second_panel, panels_two[slot * 2 * SEP:(slot + 1) * 2 * SEP], (block_row * (2 * SEP), block_col * (2 * SEP)))
                merged_schur = lax.dynamic_update_slice(merged_schur, merged[slot * 2 * SEP:(slot + 1) * 2 * SEP], (block_row * (2 * SEP), block_col * (8 * SEP)))
        return (first_factor, first_panel, second_factor, second_panel, merged_schur)
    results = lax.fori_loop(0, PAIR_ROWS * PAIR_COLS, one_group, outputs_init)
    first_factor, first_panel, second_factor, second_panel, merged_schur = results
    return (first_factor, first_panel, second_factor, second_panel, merged_schur)
```

```python
import jax
import jax.numpy as jnp
from jax import lax
from jax.experimental import pallas as pl
from jax.experimental.pallas import tpu as pltpu
from jax.sharding import PartitionSpec as P

SEP = 256
STEP = 64
HALF = 128
MESH = pl.DeviceIdType.MESH
NN = ((1,), (0,))
NT = ((1,), (1,))
TN = ((0,), (0,))
F32 = jnp.float32
B16 = jnp.bfloat16


def halves(x):
    high = x.astype(B16)
    low = (x - high.astype(F32)).astype(B16)
    return high, low


def mm(a, b, dims):
    return lax.dot_general(a, b, (dims, ((), ())), preferred_element_type=F32)


def mm3(a, b, dims):
    a_high, a_low = halves(a)
    b_high, b_low = halves(b)
    return mm(a_high, b_high, dims) + (mm(a_high, b_low, dims) + mm(a_low, b_high, dims))


def left_parts(*pairs):
    return jnp.concatenate([part for high, low in pairs for part in (high, high, low)], axis=1)


def right_parts(*pairs):
    return jnp.concatenate([part for high, low in pairs for part in (high, low, high)], axis=1)


def eliminate(tiles):
    count = len(tiles)
    sub = lax.broadcasted_iota(jnp.int32, (8, 128), 0)
    for t in range(count):
        cols = {
            g: [jnp.broadcast_to(tiles[g][:, 8 * t + k : 8 * t + k + 1], (8, 128)) for k in range(8)]
            for g in range(t, count)
        }
        for k in range(8):
            scale = lax.rsqrt(cols[t][k][k : k + 1, :])
            final_row = tiles[t][k : k + 1, :] * scale
            diag_row = [cols[t][m][k : k + 1, :] * scale for m in range(k + 1, 8)]
            for g in range(t, count):
                factor = cols[g][k] * scale
                if g == t:
                    factor = jnp.where(sub > k, factor, 0.0)
                for m in range(k + 1, 8):
                    cols[g][m] = cols[g][m] - factor * diag_row[m - k - 1]
                tiles[g] = tiles[g] - factor * final_row
            tiles[t] = jnp.where(sub == k, final_row, tiles[t])
    return tiles


def factor_panels(work, n, service):
    lane = lax.broadcasted_iota(jnp.int32, (STEP, 128), 1)
    eye = jnp.where(lane == lax.broadcasted_iota(jnp.int32, (STEP, 128), 0) + STEP, 1.0, 0.0)

    def panel(p, carry):
        start = pl.multiple_of(p * STEP, STEP)
        base = pl.multiple_of((p // 2) * 128, 128)
        block = work[pl.ds(start, STEP), pl.ds(base, 128)]
        block = jnp.where(p % 2 == 0, block, pltpu.roll(block, STEP, 1))
        block = jnp.where(lane < STEP, block, eye)
        tiles = eliminate([block[8 * g : 8 * g + 8, :] for g in range(STEP // 8)])
        inverse = jnp.concatenate(tiles, axis=0)[:, STEP:]
        strip = mm3(inverse, work[pl.ds(start, STEP), :], NN)
        work[pl.ds(start, STEP), :] = strip
        s_high, s_low = halves(strip)
        column = lax.broadcasted_iota(jnp.int32, (STEP, n), 1)
        c_high, c_low = halves(jnp.where(column >= start + STEP, strip[:, :n], 0.0))
        left = jnp.concatenate([c_high, c_high, c_low, c_low], axis=0)
        right = jnp.concatenate([s_high, s_low, s_high, s_low], axis=0)
        work[...] -= mm(left, right, TN)
        for when in service:
            pl.when(p == when)(service[when])
        return carry

    lax.fori_loop(0, n // STEP, panel, 0)


def load_pivot(q, order_row, work):
    n = q.shape[0]
    order_col = jnp.broadcast_to(order_row.astype(F32), (8, n)).T[:, :1]
    column = lax.broadcasted_iota(jnp.int32, (n, n), 1).astype(F32)
    pick = jnp.where(column == order_col, 1.0, 0.0)
    pick16 = pick.astype(B16)
    q_high, q_low = halves(q)
    rows = mm(pick16, q_high, NN) + mm(pick16, q_low, NN)
    r_high, r_low = halves(rows)
    work[:, :n] = mm(r_high, pick16, NT) + mm(r_low, pick16, NT)
    work[:, n:] = pick


def pack(full, ref):
    row = lax.broadcasted_iota(jnp.int32, (HALF, HALF), 0)
    col = lax.broadcasted_iota(jnp.int32, (HALF, HALF), 1)
    last = full[HALF:, HALF:]
    ref[:HALF] = jnp.where(row >= col, full[:HALF, :HALF], last)
    ref[HALF : 2 * HALF] = full[HALF:, :HALF]
    diagonal = jnp.sum(jnp.where(row == col, last, 0.0), axis=0, keepdims=True)
    ref[2 * HALF :] = jnp.broadcast_to(diagonal, (8, HALF))


def unpack(packed):
    row = lax.broadcasted_iota(jnp.int32, (HALF, HALF), 0)
    col = lax.broadcasted_iota(jnp.int32, (HALF, HALF), 1)
    mixed, side, diagonal = packed[:HALF], packed[HALF : 2 * HALF], packed[2 * HALF : 2 * HALF + 1]
    turned = mixed.T
    first = jnp.where(row >= col, mixed, turned)
    last = jnp.where(row < col, mixed, jnp.where(row == col, diagonal, turned))
    return jnp.concatenate(
        [jnp.concatenate([first, side.T], axis=1), jnp.concatenate([side, last], axis=1)], axis=0
    )


def new_targets(slots, left_side, upper_side):
    edge_index = slots // SEP
    west_pos = jnp.where(left_side, 1, 0).astype(jnp.int32)
    north_pos = jnp.where(upper_side, 2, 3).astype(jnp.int32)
    new_edge = jnp.where(
        edge_index == 0,
        west_pos,
        jnp.where(
            edge_index == 1, 1 - west_pos, jnp.where(edge_index == 2, north_pos, 5 - north_pos)
        ),
    )
    return new_edge * SEP + slots % SEP


PACKED = 2 * HALF + 8
NAMES = (
    "shared", "couple_in", "couple_out", "corner_sum", "in0_pass", "in1_pass", "raw_top_pass",
    "raw_side", "low0_pass", "low1_pass", "out0_pass", "out1_pass", "out2_pass", "out3_pass",
    "raw_top", "corner", "in0", "in1", "low0", "low1", "out0", "out1", "out2", "out3",
)
Y_COUNT = 14
AFTER_IN = ('low1', 'raw_side')
PLAN = {0: ((), ('out0',)), 2: (('low0',), ('low0_pass', 'out1')), 4: (('low1',), ('low1_pass', 'out2')), 6: (('out0',), ('out0_pass', 'out3'))}
PLAN_A = (('out1',), ('out1_pass',))
PLAN_B = ((), ())


def kernel(
    schur, slots_in, order_one_in, order_two_in,
    first_factor, first_panel, second_factor, second_panel, near, own_high, own_low, far_high, far_low,
    block, slots, order_one, order_two, a_high, a_low, picks, g_high, g_low,
    shared, shared_o, corner, corner_f, corner_s, corner_o,
    couple, couple_o, raw, raw_o, raw_f, raw_fo,
    panel, panel_o, inner_f, inner_fo, outer_f, outer_fo,
    sides, pivot, work_one, work_two, maps, flag,
    load_sem, send_sem, recv_sem,
):
    rows = lax.axis_size("gx")
    cols = lax.axis_size("gy")
    pair_rows, pair_cols = rows // 2, cols // 2
    r, c = lax.axis_index("gx"), lax.axis_index("gy")
    row_high, col_high = r // pair_rows, c // pair_cols
    upper, left = r < pair_rows, c < pair_cols
    pair_row, pair_col = r % pair_rows, c % pair_cols
    row_peer = (lax.rem(r + pair_rows, rows), c)
    col_peer = (r, lax.rem(c + pair_cols, cols))

    barrier = pltpu.get_barrier_semaphore()
    for peer in (row_peer, col_peer):
        pl.semaphore_signal(barrier, inc=1, device_id=peer, device_id_type=MESH)

    def part(ref, start, size):
        return ref.at[pl.ds(start, size)]

    ends = {
        "shared": (shared, shared_o),
        "couple_in": (part(couple, 0, 256), part(couple_o, 0, 256)),
        "couple_out": (part(couple, 256, 512), part(couple_o, 256, 512)),
        "corner_sum": (corner_s, corner_o),
        "raw_top_pass": (part(raw_f, 0, 256), part(raw_fo, 0, 256)),
        "raw_side": (raw, raw_o),
        "raw_top": (part(raw, 0, 256), part(raw_f, 0, 256)),
        "corner": (corner, corner_f),
    }
    for i in range(2):
        ends[f"in{i}_pass"] = (part(inner_f, 128 * i, 128), part(inner_fo, 128 * i, 128))
        ends[f"low{i}_pass"] = (part(raw_f, 256 + 128 * i, 128), part(raw_fo, 256 + 128 * i, 128))
        ends[f"in{i}"] = (part(panel, 128 * i, 128), part(inner_f, 128 * i, 128))
        ends[f"low{i}"] = (part(raw, 256 + 128 * i, 128), part(raw_f, 256 + 128 * i, 128))
    for i in range(4):
        ends[f"out{i}_pass"] = (part(outer_f, 128 * i, 128), part(outer_fo, 128 * i, 128))
        ends[f"out{i}"] = (part(panel, 256 + 128 * i, 128), part(outer_f, 128 * i, 128))

    def move(name):
        k = NAMES.index(name)
        return pltpu.make_async_remote_copy(
            src_ref=ends[name][0],
            dst_ref=ends[name][1],
            send_sem=send_sem.at[k],
            recv_sem=recv_sem.at[k],
            device_id=row_peer if k < Y_COUNT else col_peer,
            device_id_type=MESH,
        )

    def fence():
        def mark(i, carry):
            flag[...] = jnp.zeros_like(flag)
            return carry

        lax.fori_loop(0, jnp.minimum(r, 0), mark, 0)

    def send(*names):
        for name in names:
            move(name).start()
        fence()

    def arrived(*names):
        for name in names:
            move(name).wait_recv()

    small = [
        pltpu.make_async_copy(src, dst, load_sem.at[4 + i])
        for i, (src, dst) in enumerate(
            ((slots_in, slots), (order_one_in, order_one), (order_two_in, order_two))
        )
    ]
    loads = [
        pltpu.make_async_copy(part(schur, 256 * i, 256), part(block, 256 * i, 256), load_sem.at[i])
        for i in range(4)
    ]
    for load in small + loads:
        load.start()
    fence()
    small[0].wait()

    target = new_targets(slots[0], left, upper)
    for i, s in enumerate((0, 3, 1, 2)):
        rank = lax.broadcasted_iota(jnp.int32, (SEP, 4 * SEP), 0) + s * SEP
        picks[i * SEP : (i + 1) * SEP, :] = jnp.where(rank == target, 1.0, 0.0).astype(B16)
    spots = {0: 0, 3: SEP, 1: 2 * SEP, 2: 3 * SEP}

    def gather(start, stop, first):
        chosen = picks[spots[first] : spots[first] + 2 * SEP]
        g_high[start:stop] = mm(a_high[start:stop], chosen, NT).astype(B16)
        g_low[start:stop] = mm(a_low[start:stop], chosen, NT).astype(B16)

    for i in range(4):
        loads[i].wait()
        spot = slice(i * SEP, (i + 1) * SEP)
        a_high[spot], a_low[spot] = halves(block[spot])
        gather(i * SEP, (i + 1) * SEP, 0)

    def picked(s, count, first, width=SEP):
        chosen = picks[spots[s] : spots[s] + count * SEP]
        return mm(chosen, g_high[:, first : first + width], NN) + mm(
            chosen, g_low[:, first : first + width], NN
        )

    raw[:SEP] = picked(1, 1, 0)
    pack(picked(3, 1, SEP), shared)
    pl.semaphore_wait(barrier, 2)
    send("shared", "raw_top")
    pack(picked(0, 1, 0), corner)
    couple[:SEP] = picked(0, 1, SEP)
    send("corner", "couple_in")
    couple[SEP:] = picked(1, 2, SEP)
    send("couple_out")
    raw[SEP:] = picked(2, 1, 0)
    gather(0, 4 * SEP, 1)
    near[:, : 2 * SEP] = picked(1, 2, 0, 2 * SEP)
    for load in small[1:]:
        load.wait()

    arrived("shared")
    load_pivot(unpack(shared[...] + shared_o[...]), order_one[pl.ds(pair_row, 1), 0, :], work_one)
    factor_panels(work_one, SEP, {})
    inverse = halves(work_one[:, SEP:])

    def panel_of(coupling):
        return mm(left_parts(halves(coupling)), right_parts(inverse), NT)

    panel[:SEP] = panel_of(couple[:SEP])
    send("in0", "in1")
    panel[SEP:] = panel_of(couple[SEP:])
    arrived("couple_in")
    panel_o[:SEP] = panel_of(couple_o[:SEP])
    mine = pl.ds(pl.multiple_of(row_high * SEP, SEP), SEP)
    theirs = pl.ds(pl.multiple_of((1 - row_high) * SEP, SEP), SEP)
    sides[mine, :SEP] = panel[:SEP]
    sides[theirs, :SEP] = panel_o[:SEP]

    def gram(x):
        pair = halves(x)
        return mm(left_parts(pair), right_parts(pair), NT)

    pivot[...] = -gram(sides[:, :SEP])
    arrived("corner")
    corner_s[...] = corner[...] + corner_f[...]
    send("corner_sum")
    upper_rows = work_one[:, pl.ds(pl.multiple_of(row_high * HALF, HALF), HALF)]
    row = lax.broadcasted_iota(jnp.int32, (SEP, HALF), 0)
    col = lax.broadcasted_iota(jnp.int32, (SEP, HALF), 1) + row_high * HALF
    first_factor[...] = jnp.where(row <= col, upper_rows, 0.0).T
    first_panel[...] = panel[...]
    arrived("couple_out")
    panel_o[SEP:] = panel_of(couple_o[SEP:])
    outer = halves(panel[SEP:])
    outer_o = halves(panel_o[SEP:])
    near[:, : 2 * SEP] -= mm(left_parts(outer), right_parts(outer), NT)
    near[:, 2 * SEP :] = -mm(left_parts(outer), right_parts(outer_o), NT)
    arrived("in0")
    send("in0_pass")
    arrived("in1")
    send("in1_pass", "low0")
    arrived("raw_top")
    send("raw_top_pass")
    sides[mine, SEP:] = inner_f[...]
    arrived("corner_sum")
    pivot[mine, mine] += unpack(corner_s[...])
    pivot[theirs, theirs] += unpack(corner_o[...])
    arrived("in0_pass", "in1_pass")
    send(*AFTER_IN)
    sides[theirs, SEP:] = inner_fo[...]
    n = 2 * SEP
    order = order_two[pair_row]
    rank = lax.broadcasted_iota(jnp.int32, order.shape, 0)
    order = jnp.sum(jnp.where(rank == pair_col, order.astype(F32), 0.0), axis=0, keepdims=True)
    load_pivot(pivot[...] - gram(sides[:, SEP:]), order, work_two)

    def step(got, sent):
        def run():
            arrived(*got)
            if sent:
                send(*sent)

        return run

    factor_panels(work_two, n, {when: step(*lists) for when, lists in PLAN.items()})
    inverse_two = halves(work_two[:, n:])
    s_high, s_low = halves(sides[...])
    maps[...] = -mm(
        left_parts(inverse_two), jnp.concatenate([s_high, s_low, s_high], axis=0), NN
    )
    step(*PLAN_A)()
    mine_two = pl.ds(pl.multiple_of(n + row_high * SEP, SEP), SEP)
    theirs_two = pl.ds(pl.multiple_of(n + (1 - row_high) * SEP, SEP), SEP)
    own_maps = right_parts(halves(work_two[:, mine_two]), halves(maps[:, :SEP]))
    second = mm(left_parts(halves(raw[...]), halves(panel[SEP:])), own_maps, NT)
    second_panel[...] = second
    own_high[...], own_low[...] = halves(second)
    own = (own_high[...], own_low[...])
    near[:, :n] -= mm(left_parts(own), right_parts(own), NT)
    step(*PLAN_B)()
    arrived("raw_side")
    other_maps = right_parts(halves(work_two[:, theirs_two]), halves(maps[:, :SEP]))
    outer_o = halves(panel_o[SEP:])
    second_o = halves(mm(left_parts(halves(raw_o[...]), outer_o), other_maps, NT))
    near[:, n:] -= mm(left_parts(own), right_parts(second_o), NT)

    lower_rows = work_two[
        pl.ds(pl.multiple_of(col_high * SEP, SEP), SEP), pl.ds(pl.multiple_of(row_high * SEP, SEP), SEP)
    ]
    row = lax.broadcasted_iota(jnp.int32, (SEP, SEP), 0) + col_high * SEP
    col = lax.broadcasted_iota(jnp.int32, (SEP, SEP), 1) + row_high * SEP
    second_factor[...] = jnp.where(row <= col, lower_rows, 0.0).T

    far_maps = right_parts(halves(work_two[:, mine_two]), halves(maps[:, SEP:]))
    far_other_maps = right_parts(halves(work_two[:, theirs_two]), halves(maps[:, SEP:]))

    def far(start, size, raw_ref, outer_ref, map_parts, base):
        spot = slice(start, start + size)
        place = slice(base + start, base + start + size)
        rows_far = mm(left_parts(halves(raw_ref[spot]), halves(outer_ref[spot])), map_parts, NT)
        far_high[place], far_low[place] = halves(rows_far)

    far(0, SEP, raw_f, outer_f, far_maps, 0)
    arrived("out2")
    send("out2_pass")
    arrived("raw_top_pass", "out0_pass", "out1_pass")
    far(0, SEP, raw_fo, outer_fo, far_other_maps, n)
    far(SEP, HALF, raw_f, outer_f, far_maps, 0)
    arrived("out3")
    send("out3_pass")
    far(SEP + HALF, HALF, raw_f, outer_f, far_maps, 0)
    arrived("low0_pass", "low1_pass", "out2_pass")
    far(SEP, HALF, raw_fo, outer_fo, far_other_maps, n)
    arrived("out3_pass")
    far(SEP + HALF, HALF, raw_fo, outer_fo, far_other_maps, n)
    for name in NAMES:
        move(name).wait_send()


def finish(
    first_factor, first_panel, second_factor, second_panel, near, own_high, own_low, far_high, far_low,
    out_ff, out_fp, out_sf, out_sp, out_merged, piece, sems,
):
    pair_rows, pair_cols = lax.axis_size("gx") // 2, lax.axis_size("gy") // 2
    row_high, col_high = lax.axis_index("gx") // pair_rows, lax.axis_index("gy") // pair_cols
    n = 2 * SEP

    def columns(number):
        return out_merged.at[:, pl.ds(pl.multiple_of(number * n, n), n)]

    own_slot = 2 * col_high + row_high
    other_slot = 2 * col_high + 1 - row_high
    far_slots = (2 * (1 - col_high) + row_high, 2 * (1 - col_high) + 1 - row_high)
    copies = [
        (near.at[:, :n], columns(own_slot)),
        (near.at[:, n:], columns(other_slot)),
        (second_panel, out_sp),
        (first_panel, out_fp),
        (first_factor, out_ff),
        (second_factor, out_sf),
    ]
    copies = [pltpu.make_async_copy(src, dst, sems.at[i]) for i, (src, dst) in enumerate(copies)]
    for copy in copies:
        copy.start()
    own = left_parts((own_high[...], own_low[...]))
    for i in range(2):
        spot = slice(i * n, (i + 1) * n)
        piece[i] = -mm(own, right_parts((far_high[spot], far_low[spot])), NT)
        copy = pltpu.make_async_copy(piece.at[i], columns(far_slots[i]), sems.at[len(copies)])
        copy.start()
        copies.append(copy)
    for copy in copies:
        copy.wait()


VM = pl.BlockSpec(memory_space=pltpu.VMEM)


def out(*dims):
    return jax.ShapeDtypeStruct(dims, F32)


def out16(*dims):
    return jax.ShapeDtypeStruct(dims, B16)


ANY = pl.BlockSpec(memory_space=pltpu.HBM)


def body(local_schur, boundary_map, order_first, order_second):
    def f32(*dims):
        return pltpu.VMEM(dims, F32)

    def b16(*dims):
        return pltpu.VMEM(dims, B16)

    def i32(shape):
        return pltpu.VMEM(shape, jnp.int32)

    count = len(NAMES)
    factors = (
        out(SEP // 2, SEP), out(3 * SEP, SEP), out(SEP, SEP), out(2 * SEP, 2 * SEP)
    )
    results = pl.pallas_call(
        kernel,
        out_shape=factors + (
            out(2 * SEP, 4 * SEP), out16(512, 512), out16(512, 512), out16(1024, 512), out16(1024, 512)
        ),
        in_specs=[ANY] * 4,
        out_specs=(VM,) * 9,
        scratch_shapes=[
            f32(1024, 1024), i32(boundary_map.shape), i32(order_first.shape), i32(order_second.shape),
            b16(1024, 1024), b16(1024, 1024), b16(1024, 1024), b16(1024, 512), b16(1024, 512),
            f32(PACKED, HALF), f32(PACKED, HALF), f32(PACKED, HALF), f32(PACKED, HALF), f32(PACKED, HALF), f32(PACKED, HALF),
            f32(768, 256), f32(768, 256), f32(512, 256), f32(512, 256), f32(512, 256), f32(512, 256),
            f32(768, 256), f32(768, 256), f32(256, 256), f32(256, 256), f32(512, 256), f32(512, 256),
            f32(512, 512), f32(512, 512), f32(256, 512), f32(512, 1024), f32(512, 512), f32(8, 128),
            pltpu.SemaphoreType.DMA((7,)), pltpu.SemaphoreType.DMA((count,)), pltpu.SemaphoreType.DMA((count,)),
        ],
        compiler_params=pltpu.CompilerParams(
            collective_id=0, has_side_effects=True, vmem_limit_bytes=44 << 20
        ),
        cost_estimate=pl.CostEstimate(
            flops=20_000_000_000, bytes_accessed=12 << 20, transcendentals=0
        ),
    )(local_schur, boundary_map, order_first, order_second)
    return pl.pallas_call(
        finish,
        out_shape=factors + (out(2 * SEP, 8 * SEP),),
        in_specs=[VM] * 9,
        out_specs=(ANY,) * 5,
        scratch_shapes=[f32(2, 512, 512), pltpu.SemaphoreType.DMA((8,))],
        compiler_params=pltpu.CompilerParams(vmem_limit_bytes=16 << 20),
        cost_estimate=pl.CostEstimate(
            flops=2_000_000_000, bytes_accessed=12 << 20, transcendentals=0
        ),
    )(*results)


def solution(mesh):
    in_specs = (P("gx", "gy"), P("gx", "gy", None), P(None, "gy", None), P())
    out_specs = (P("gx", "gy"),) * 5
    return jax.shard_map(body, mesh=mesh, in_specs=in_specs, out_specs=out_specs, check_vma=False)
```

```python
import jax
import jax.numpy as jnp
from jax import lax
from jax.experimental import pallas as pl
from jax.experimental.pallas import tpu as pltpu
from jax.sharding import PartitionSpec as P

SEP = 256
STEP = 64
HALF = 128
MESH = pl.DeviceIdType.MESH
NN = ((1,), (0,))
NT = ((1,), (1,))
TN = ((0,), (0,))
F32 = jnp.float32
B16 = jnp.bfloat16


def halves(x):
    high = x.astype(B16)
    low = (x - high.astype(F32)).astype(B16)
    return high, low


def mm(a, b, dims):
    return lax.dot_general(a, b, (dims, ((), ())), preferred_element_type=F32)


def mm3(a, b, dims):
    a_high, a_low = halves(a)
    b_high, b_low = halves(b)
    return mm(a_high, b_high, dims) + (mm(a_high, b_low, dims) + mm(a_low, b_high, dims))


def left_parts(*pairs):
    return jnp.concatenate([part for high, low in pairs for part in (high, high, low)], axis=1)


def right_parts(*pairs):
    return jnp.concatenate([part for high, low in pairs for part in (high, low, high)], axis=1)


def eliminate(tiles):
    count = len(tiles)
    sub = lax.broadcasted_iota(jnp.int32, (8, 128), 0)
    for t in range(count):
        cols = {
            g: [jnp.broadcast_to(tiles[g][:, 8 * t + k : 8 * t + k + 1], (8, 128)) for k in range(8)]
            for g in range(t, count)
        }
        for k in range(8):
            scale = lax.rsqrt(cols[t][k][k : k + 1, :])
            final_row = tiles[t][k : k + 1, :] * scale
            diag_row = [cols[t][m][k : k + 1, :] * scale for m in range(k + 1, 8)]
            for g in range(t, count):
                factor = cols[g][k] * scale
                if g == t:
                    factor = jnp.where(sub > k, factor, 0.0)
                for m in range(k + 1, 8):
                    cols[g][m] = cols[g][m] - factor * diag_row[m - k - 1]
                tiles[g] = tiles[g] - factor * final_row
            tiles[t] = jnp.where(sub == k, final_row, tiles[t])
    return tiles


def factor_panels(work, lefts, rights, n, service):
    lane = lax.broadcasted_iota(jnp.int32, (STEP, 128), 1)
    eye = jnp.where(lane == lax.broadcasted_iota(jnp.int32, (STEP, 128), 0) + STEP, 1.0, 0.0)
    lefts[:, :n] = jnp.zeros((4 * STEP, n), B16)
    rights[:, : 2 * n] = jnp.zeros((4 * STEP, 2 * n), B16)

    def panel(p, carry):
        start = pl.multiple_of(p * STEP, STEP)
        base = pl.multiple_of((p // 2) * 128, 128)
        even = p % 2 == 0
        near_delta = mm(lefts[:, pl.ds(base, 128)], rights[:, pl.ds(base, 128)], TN)
        block = work[pl.ds(start, STEP), pl.ds(base, 128)]
        block = block - jnp.where(even, near_delta[:STEP], near_delta[STEP:])
        block = jnp.where(even, block, pltpu.roll(block, STEP, 1))
        block = jnp.where(lane < STEP, block, eye)
        work[...] -= mm(lefts[:, :n], rights[:, : 2 * n], TN)
        tiles = eliminate([block[8 * g : 8 * g + 8, :] for g in range(STEP // 8)])
        inverse = jnp.concatenate(tiles, axis=0)[:, STEP:]
        strip = mm3(inverse, work[pl.ds(start, STEP), :], NN)
        work[pl.ds(start, STEP), :] = strip
        s_high, s_low = halves(strip)
        column = lax.broadcasted_iota(jnp.int32, (STEP, n), 1)
        c_high, c_low = halves(jnp.where(column >= start + STEP, strip[:, :n], 0.0))
        lefts[:, :n] = jnp.concatenate([c_high, c_high, c_low, c_low], axis=0)
        rights[:, : 2 * n] = jnp.concatenate([s_high, s_low, s_high, s_low], axis=0)
        for when in service:
            pl.when(p == when)(service[when])
        return carry

    lax.fori_loop(0, n // STEP, panel, 0)


def load_pivot(q, order_row, work):
    n = q.shape[0]
    order_col = jnp.broadcast_to(order_row.astype(F32), (8, n)).T[:, :1]
    column = lax.broadcasted_iota(jnp.int32, (n, n), 1).astype(F32)
    pick = jnp.where(column == order_col, 1.0, 0.0)
    pick16 = pick.astype(B16)
    q_high, q_low = halves(q)
    rows = mm(pick16, q_high, NN) + mm(pick16, q_low, NN)
    r_high, r_low = halves(rows)
    work[:, :n] = mm(r_high, pick16, NT) + mm(r_low, pick16, NT)
    work[:, n:] = pick


def pack(full, ref):
    row = lax.broadcasted_iota(jnp.int32, (HALF, HALF), 0)
    col = lax.broadcasted_iota(jnp.int32, (HALF, HALF), 1)
    last = full[HALF:, HALF:]
    ref[:HALF] = jnp.where(row >= col, full[:HALF, :HALF], last)
    ref[HALF : 2 * HALF] = full[HALF:, :HALF]
    diagonal = jnp.sum(jnp.where(row == col, last, 0.0), axis=0, keepdims=True)
    ref[2 * HALF :] = jnp.broadcast_to(diagonal, (8, HALF))


def unpack(packed):
    row = lax.broadcasted_iota(jnp.int32, (HALF, HALF), 0)
    col = lax.broadcasted_iota(jnp.int32, (HALF, HALF), 1)
    mixed, side, diagonal = packed[:HALF], packed[HALF : 2 * HALF], packed[2 * HALF : 2 * HALF + 1]
    turned = mixed.T
    first = jnp.where(row >= col, mixed, turned)
    last = jnp.where(row < col, mixed, jnp.where(row == col, diagonal, turned))
    return jnp.concatenate(
        [jnp.concatenate([first, side.T], axis=1), jnp.concatenate([side, last], axis=1)], axis=0
    )


def new_targets(slots, left_side, upper_side):
    edge_index = slots // SEP
    west_pos = jnp.where(left_side, 1, 0).astype(jnp.int32)
    north_pos = jnp.where(upper_side, 2, 3).astype(jnp.int32)
    new_edge = jnp.where(
        edge_index == 0,
        west_pos,
        jnp.where(
            edge_index == 1, 1 - west_pos, jnp.where(edge_index == 2, north_pos, 5 - north_pos)
        ),
    )
    return new_edge * SEP + slots % SEP


PACKED = 2 * HALF + 8
Y_NAMES = (
    "shared", "couple_in", "couple_out", "corner_sum", "in0_pass", "in1_pass", "in2_pass", "in3_pass",
    "raw_top_pass", "side0", "side1", "side2", "side3", "low0_pass", "low1_pass",
    "out0_pass", "out1_pass", "out2_pass", "out3_pass", "out4_pass",
)
Z_NAMES = (
    "raw_top", "corner", "in0", "in1", "in2", "in3", "low0", "low1",
    "out0", "out1", "out2", "out3", "out4",
)
NAMES = Y_NAMES + Z_NAMES
Y_COUNT = len(Y_NAMES)
OUTER = ((0, 128), (128, 128), (256, 128), (384, 64), (448, 64))
AFTER_IN = ('low1', 'side0', 'side1', 'side2', 'side3')
PLAN = {0: ((), ('out0',)), 2: (('low0',), ('low0_pass', 'out1')), 4: (('low1',), ('low1_pass', 'out2')), 6: (('out0',), ('out0_pass', 'out3', 'out4'))}
PLAN_A = (('out1',), ('out1_pass',))
PLAN_B = ((), ())


def kernel(
    schur, table,
    first_factor, first_panel, second_factor, second_panel, near, own_high, own_low, far_high, far_low,
    block, a_high, a_low, picks, g_high, g_low,
    shared, shared_o, corner, corner_f, corner_s, corner_o,
    couple, couple_o, raw, raw_o, raw_f, raw_fo,
    panel, panel_o, inner_f, inner_fo, outer_f, outer_fo,
    sides, pivot, work_one, work_two, maps, flag, lefts, rights,
    load_sem, send_sem, recv_sem,
):
    rows = lax.axis_size("gx")
    cols = lax.axis_size("gy")
    pair_rows, pair_cols = rows // 2, cols // 2
    r, c = lax.axis_index("gx"), lax.axis_index("gy")
    row_high, col_high = r // pair_rows, c // pair_cols
    upper, left = r < pair_rows, c < pair_cols
    pair_row, pair_col = r % pair_rows, c % pair_cols
    row_peer = (lax.rem(r + pair_rows, rows), c)
    col_peer = (r, lax.rem(c + pair_cols, cols))

    barrier = pltpu.get_barrier_semaphore()
    for peer in (row_peer, col_peer):
        pl.semaphore_signal(barrier, inc=1, device_id=peer, device_id_type=MESH)

    def part(ref, start, size):
        return ref.at[pl.ds(start, size)]

    ends = {
        "shared": (shared, shared_o),
        "couple_in": (part(couple, 0, 256), part(couple_o, 0, 256)),
        "couple_out": (part(couple, 256, 512), part(couple_o, 256, 512)),
        "corner_sum": (corner_s, corner_o),
        "raw_top_pass": (part(raw_f, 0, 256), part(raw_fo, 0, 256)),
        "raw_top": (part(raw, 0, 256), part(raw_f, 0, 256)),
        "corner": (corner, corner_f),
    }
    for i in range(2):
        ends[f"low{i}_pass"] = (part(raw_f, 256 + 128 * i, 128), part(raw_fo, 256 + 128 * i, 128))
        ends[f"low{i}"] = (part(raw, 256 + 128 * i, 128), part(raw_f, 256 + 128 * i, 128))
    for i in range(4):
        ends[f"in{i}_pass"] = (part(inner_f, 64 * i, 64), part(inner_fo, 64 * i, 64))
        ends[f"in{i}"] = (part(panel, 64 * i, 64), part(inner_f, 64 * i, 64))
        ends[f"side{i}"] = (part(raw, 128 * i, 128), part(raw_o, 128 * i, 128))
    for i, (start, size) in enumerate(OUTER):
        ends[f"out{i}_pass"] = (part(outer_f, start, size), part(outer_fo, start, size))
        ends[f"out{i}"] = (part(panel, 256 + start, size), part(outer_f, start, size))

    def move(name):
        k = NAMES.index(name)
        return pltpu.make_async_remote_copy(
            src_ref=ends[name][0],
            dst_ref=ends[name][1],
            send_sem=send_sem.at[k],
            recv_sem=recv_sem.at[k],
            device_id=row_peer if k < Y_COUNT else col_peer,
            device_id_type=MESH,
        )

    def fence():
        def mark(i, carry):
            flag[...] = jnp.zeros_like(flag)
            return carry

        lax.fori_loop(0, jnp.minimum(r, 0), mark, 0)

    def send(*names):
        for name in names:
            move(name).start()
        fence()

    def arrived(*names):
        for name in names:
            move(name).wait_recv()

    loads = [
        pltpu.make_async_copy(part(schur, 256 * i, 256), part(block, 256 * i, 256), load_sem.at[i])
        for i in range(4)
    ]
    for load in loads:
        load.start()
    fence()

    def listed(first, count, stride=1):
        return jnp.concatenate(
            [table[pl.ds(first + stride * i, 1), :] for i in range(count)], axis=1
        )

    target = new_targets(listed(0, 8), left, upper)
    for i, s in enumerate((0, 3, 1, 2)):
        rank = lax.broadcasted_iota(jnp.int32, (SEP, 4 * SEP), 0) + s * SEP
        picks[i * SEP : (i + 1) * SEP, :] = jnp.where(rank == target, 1.0, 0.0).astype(B16)
    spots = {0: 0, 3: SEP, 1: 2 * SEP, 2: 3 * SEP}

    def gather(start, stop, first):
        chosen = picks[spots[first] : spots[first] + 2 * SEP]
        g_high[start:stop] = mm(a_high[start:stop], chosen, NT).astype(B16)
        g_low[start:stop] = mm(a_low[start:stop], chosen, NT).astype(B16)

    for i in range(4):
        loads[i].wait()
        spot = slice(i * SEP, (i + 1) * SEP)
        a_high[spot], a_low[spot] = halves(block[spot])
        gather(i * SEP, (i + 1) * SEP, 0)

    def picked(s, count, first, width=SEP):
        chosen = picks[spots[s] : spots[s] + count * SEP]
        return mm(chosen, g_high[:, first : first + width], NN) + mm(
            chosen, g_low[:, first : first + width], NN
        )

    raw[:SEP] = picked(1, 1, 0)
    pack(picked(3, 1, SEP), shared)
    pl.semaphore_wait(barrier, 2)
    send("shared", "raw_top")
    pack(picked(0, 1, 0), corner)
    couple[:SEP] = picked(0, 1, SEP)
    send("corner", "couple_in")
    couple[SEP:] = picked(1, 2, SEP)
    send("couple_out")
    raw[SEP:] = picked(2, 1, 0)
    gather(0, 4 * SEP, 1)
    near[:, : 2 * SEP] = picked(1, 2, 0, 2 * SEP)

    arrived("shared")
    load_pivot(unpack(shared[...] + shared_o[...]), listed(8 + 2 * pair_row, 2), work_one)
    factor_panels(work_one, lefts, rights, SEP, {})
    inverse = halves(work_one[:, SEP:])

    def panel_of(coupling):
        return mm(left_parts(halves(coupling)), right_parts(inverse), NT)

    panel[:SEP] = panel_of(couple[:SEP])
    send("in0", "in1", "in2", "in3")
    panel[SEP:] = panel_of(couple[SEP:])
    arrived("couple_in")
    panel_o[:SEP] = panel_of(couple_o[:SEP])
    mine = pl.ds(pl.multiple_of(row_high * SEP, SEP), SEP)
    theirs = pl.ds(pl.multiple_of((1 - row_high) * SEP, SEP), SEP)
    sides[mine, :SEP] = panel[:SEP]
    sides[theirs, :SEP] = panel_o[:SEP]

    def gram(x):
        pair = halves(x)
        return mm(left_parts(pair), right_parts(pair), NT)

    pivot[...] = -gram(sides[:, :SEP])
    arrived("corner")
    corner_s[...] = corner[...] + corner_f[...]
    send("corner_sum")
    upper_rows = work_one[:, pl.ds(pl.multiple_of(row_high * HALF, HALF), HALF)]
    row = lax.broadcasted_iota(jnp.int32, (SEP, HALF), 0)
    col = lax.broadcasted_iota(jnp.int32, (SEP, HALF), 1) + row_high * HALF
    first_factor[...] = jnp.where(row <= col, upper_rows, 0.0).T
    first_panel[...] = panel[...]
    arrived("couple_out")
    panel_o[SEP:] = panel_of(couple_o[SEP:])
    outer = halves(panel[SEP:])
    outer_o = halves(panel_o[SEP:])
    near[:, : 2 * SEP] -= mm(left_parts(outer), right_parts(outer), NT)
    near[:, 2 * SEP :] = -mm(left_parts(outer), right_parts(outer_o), NT)
    arrived("in0")
    send("in0_pass")
    arrived("in1")
    send("in1_pass")
    arrived("in2")
    send("in2_pass")
    arrived("in3")
    send("in3_pass", "low0")
    arrived("raw_top")
    send("raw_top_pass")
    sides[mine, SEP:] = inner_f[...]
    arrived("corner_sum")
    pivot[mine, mine] += unpack(corner_s[...])
    pivot[theirs, theirs] += unpack(corner_o[...])
    arrived("in0_pass", "in1_pass", "in2_pass", "in3_pass")
    send(*AFTER_IN)
    sides[theirs, SEP:] = inner_fo[...]
    n = 2 * SEP
    order = listed(8 + 2 * pair_rows + 4 * pair_row * pair_cols + pair_col, 4, pair_cols)
    load_pivot(pivot[...] - gram(sides[:, SEP:]), order, work_two)

    def step(got, sent):
        def run():
            arrived(*got)
            if sent:
                send(*sent)

        return run

    factor_panels(work_two, lefts, rights, n, {when: step(*lists) for when, lists in PLAN.items()})
    inverse_two = halves(work_two[:, n:])
    s_high, s_low = halves(sides[...])
    maps[...] = -mm(
        left_parts(inverse_two), jnp.concatenate([s_high, s_low, s_high], axis=0), NN
    )
    step(*PLAN_A)()
    mine_two = pl.ds(pl.multiple_of(n + row_high * SEP, SEP), SEP)
    theirs_two = pl.ds(pl.multiple_of(n + (1 - row_high) * SEP, SEP), SEP)
    own_maps = right_parts(halves(work_two[:, mine_two]), halves(maps[:, :SEP]))
    second = mm(left_parts(halves(raw[...]), halves(panel[SEP:])), own_maps, NT)
    second_panel[...] = second
    own_high[...], own_low[...] = halves(second)
    own = (own_high[...], own_low[...])
    near[:, :n] -= mm(left_parts(own), right_parts(own), NT)
    step(*PLAN_B)()
    arrived("side0", "side1", "side2", "side3")
    other_maps = right_parts(halves(work_two[:, theirs_two]), halves(maps[:, :SEP]))
    outer_o = halves(panel_o[SEP:])
    second_o = halves(mm(left_parts(halves(raw_o[...]), outer_o), other_maps, NT))
    near[:, n:] -= mm(left_parts(own), right_parts(second_o), NT)

    lower_rows = work_two[
        pl.ds(pl.multiple_of(col_high * SEP, SEP), SEP), pl.ds(pl.multiple_of(row_high * SEP, SEP), SEP)
    ]
    row = lax.broadcasted_iota(jnp.int32, (SEP, SEP), 0) + col_high * SEP
    col = lax.broadcasted_iota(jnp.int32, (SEP, SEP), 1) + row_high * SEP
    second_factor[...] = jnp.where(row <= col, lower_rows, 0.0).T

    far_maps = right_parts(halves(work_two[:, mine_two]), halves(maps[:, SEP:]))
    far_other_maps = right_parts(halves(work_two[:, theirs_two]), halves(maps[:, SEP:]))

    def far(start, size, raw_ref, outer_ref, map_parts, base):
        spot = slice(start, start + size)
        place = slice(base + start, base + start + size)
        rows_far = mm(left_parts(halves(raw_ref[spot]), halves(outer_ref[spot])), map_parts, NT)
        far_high[place], far_low[place] = halves(rows_far)

    far(0, SEP, raw_f, outer_f, far_maps, 0)
    arrived("out2")
    send("out2_pass")
    arrived("raw_top_pass", "out0_pass", "out1_pass")
    far(0, SEP, raw_fo, outer_fo, far_other_maps, n)
    far(SEP, HALF, raw_f, outer_f, far_maps, 0)
    arrived("out3")
    send("out3_pass")
    arrived("out4")
    send("out4_pass")
    far(SEP + HALF, HALF, raw_f, outer_f, far_maps, 0)
    arrived("low0_pass", "low1_pass", "out2_pass")
    far(SEP, HALF, raw_fo, outer_fo, far_other_maps, n)
    arrived("out3_pass", "out4_pass")
    far(SEP + HALF, HALF, raw_fo, outer_fo, far_other_maps, n)
    for name in NAMES:
        move(name).wait_send()


def finish(
    first_factor, first_panel, second_factor, second_panel, near, own_high, own_low, far_high, far_low,
    out_ff, out_fp, out_sf, out_sp, out_merged, piece, sems,
):
    pair_rows, pair_cols = lax.axis_size("gx") // 2, lax.axis_size("gy") // 2
    row_high, col_high = lax.axis_index("gx") // pair_rows, lax.axis_index("gy") // pair_cols
    n = 2 * SEP

    def columns(number):
        return out_merged.at[:, pl.ds(pl.multiple_of(number * n, n), n)]

    own_slot = 2 * col_high + row_high
    other_slot = 2 * col_high + 1 - row_high
    far_slots = (2 * (1 - col_high) + row_high, 2 * (1 - col_high) + 1 - row_high)
    copies = [
        (near.at[:, :n], columns(own_slot)),
        (near.at[:, n:], columns(other_slot)),
        (second_panel, out_sp),
        (first_panel, out_fp),
        (first_factor, out_ff),
        (second_factor, out_sf),
    ]
    copies = [pltpu.make_async_copy(src, dst, sems.at[i]) for i, (src, dst) in enumerate(copies)]
    for copy in copies:
        copy.start()
    own = left_parts((own_high[...], own_low[...]))
    for i in range(2):
        spot = slice(i * n, (i + 1) * n)
        piece[i] = -mm(own, right_parts((far_high[spot], far_low[spot])), NT)
        copy = pltpu.make_async_copy(piece.at[i], columns(far_slots[i]), sems.at[len(copies)])
        copy.start()
        copies.append(copy)
    for copy in copies:
        copy.wait()


VM = pl.BlockSpec(memory_space=pltpu.VMEM)


def out(*dims):
    return jax.ShapeDtypeStruct(dims, F32)


def out16(*dims):
    return jax.ShapeDtypeStruct(dims, B16)


ANY = pl.BlockSpec(memory_space=pltpu.HBM)


def body(local_schur, boundary_map, order_first, order_second):
    def f32(*dims):
        return pltpu.VMEM(dims, F32)

    def b16(*dims):
        return pltpu.VMEM(dims, B16)

    order_second = order_second.reshape(order_second.shape[:2] + (4, HALF)).transpose(0, 2, 1, 3)
    table = jnp.concatenate(
        [lines.reshape(-1, HALF) for lines in (boundary_map, order_first, order_second)], axis=0
    )
    count = len(NAMES)
    factors = (
        out(SEP // 2, SEP), out(3 * SEP, SEP), out(SEP, SEP), out(2 * SEP, 2 * SEP)
    )
    results = pl.pallas_call(
        kernel,
        out_shape=factors + (
            out(2 * SEP, 4 * SEP), out16(512, 512), out16(512, 512), out16(1024, 512), out16(1024, 512)
        ),
        in_specs=[ANY, VM],
        out_specs=(VM,) * 9,
        scratch_shapes=[
            f32(1024, 1024), b16(1024, 1024), b16(1024, 1024), b16(1024, 1024), b16(1024, 512), b16(1024, 512),
            f32(PACKED, HALF), f32(PACKED, HALF), f32(PACKED, HALF), f32(PACKED, HALF), f32(PACKED, HALF), f32(PACKED, HALF),
            f32(768, 256), f32(768, 256), f32(512, 256), f32(512, 256), f32(512, 256), f32(512, 256),
            f32(768, 256), f32(768, 256), f32(256, 256), f32(256, 256), f32(512, 256), f32(512, 256),
            f32(512, 512), f32(512, 512), f32(256, 512), f32(512, 1024), f32(512, 512), f32(8, 128), b16(256, 512), b16(256, 1024),
            pltpu.SemaphoreType.DMA((4,)), pltpu.SemaphoreType.DMA((count,)), pltpu.SemaphoreType.DMA((count,)),
        ],
        compiler_params=pltpu.CompilerParams(
            collective_id=0, has_side_effects=True, vmem_limit_bytes=44 << 20
        ),
        cost_estimate=pl.CostEstimate(
            flops=20_000_000_000, bytes_accessed=12 << 20, transcendentals=0
        ),
    )(local_schur, table)
    return pl.pallas_call(
        finish,
        out_shape=factors + (out(2 * SEP, 8 * SEP),),
        in_specs=[VM] * 9,
        out_specs=(ANY,) * 5,
        scratch_shapes=[f32(2, 512, 512), pltpu.SemaphoreType.DMA((8,))],
        compiler_params=pltpu.CompilerParams(vmem_limit_bytes=16 << 20),
        cost_estimate=pl.CostEstimate(
            flops=2_000_000_000, bytes_accessed=12 << 20, transcendentals=0
        ),
    )(*results)


def solution(mesh):
    in_specs = (P("gx", "gy"), P("gx", "gy", None), P(None, "gy", None), P())
    out_specs = (P("gx", "gy"),) * 5
    return jax.shard_map(body, mesh=mesh, in_specs=in_specs, out_specs=out_specs, check_vma=False)
```

```python
import jax
import jax.numpy as jnp
from jax import lax
from jax.experimental import pallas as pl
from jax.experimental.pallas import tpu as pltpu
from jax.sharding import PartitionSpec as P

SEP = 256
STEP = 64
HALF = 128
MESH = pl.DeviceIdType.MESH
NN = ((1,), (0,))
NT = ((1,), (1,))
TN = ((0,), (0,))
F32 = jnp.float32
B16 = jnp.bfloat16


def halves(x):
    high = x.astype(B16)
    low = (x - high.astype(F32)).astype(B16)
    return high, low


def mm(a, b, dims):
    return lax.dot_general(a, b, (dims, ((), ())), preferred_element_type=F32)


def mm3(a, b, dims):
    a_high, a_low = halves(a)
    b_high, b_low = halves(b)
    return mm(a_high, b_high, dims) + (mm(a_high, b_low, dims) + mm(a_low, b_high, dims))


def left_parts(*pairs):
    return jnp.concatenate([part for high, low in pairs for part in (high, high, low)], axis=1)


def right_parts(*pairs):
    return jnp.concatenate([part for high, low in pairs for part in (high, low, high)], axis=1)


def eliminate(tiles):
    count = len(tiles)
    sub = lax.broadcasted_iota(jnp.int32, (8, 128), 0)
    for t in range(count):
        cols = {
            g: [jnp.broadcast_to(tiles[g][:, 8 * t + k : 8 * t + k + 1], (8, 128)) for k in range(8)]
            for g in range(t, count)
        }
        for k in range(8):
            scale = lax.rsqrt(cols[t][k][k : k + 1, :])
            final_row = tiles[t][k : k + 1, :] * scale
            diag_row = [cols[t][m][k : k + 1, :] * scale for m in range(k + 1, 8)]
            for g in range(t, count):
                factor = cols[g][k] * scale
                if g == t:
                    factor = jnp.where(sub > k, factor, 0.0)
                for m in range(k + 1, 8):
                    cols[g][m] = cols[g][m] - factor * diag_row[m - k - 1]
                tiles[g] = tiles[g] - factor * final_row
            tiles[t] = jnp.where(sub == k, final_row, tiles[t])
    return tiles


def factor_panels(work, lefts, rights, n, service):
    lane = lax.broadcasted_iota(jnp.int32, (STEP, 128), 1)
    eye = jnp.where(lane == lax.broadcasted_iota(jnp.int32, (STEP, 128), 0) + STEP, 1.0, 0.0)
    lefts[:, :n] = jnp.zeros((4 * STEP, n), B16)
    rights[:, : 2 * n] = jnp.zeros((4 * STEP, 2 * n), B16)

    def panel(p, carry):
        start = pl.multiple_of(p * STEP, STEP)
        base = pl.multiple_of((p // 2) * 128, 128)
        even = p % 2 == 0
        near_delta = mm(lefts[:, pl.ds(base, 128)], rights[:, pl.ds(base, 128)], TN)
        block = work[pl.ds(start, STEP), pl.ds(base, 128)]
        block = block - jnp.where(even, near_delta[:STEP], near_delta[STEP:])
        block = jnp.where(even, block, pltpu.roll(block, STEP, 1))
        block = jnp.where(lane < STEP, block, eye)
        work[...] -= mm(lefts[:, :n], rights[:, : 2 * n], TN)
        tiles = eliminate([block[8 * g : 8 * g + 8, :] for g in range(STEP // 8)])
        inverse = jnp.concatenate(tiles, axis=0)[:, STEP:]
        strip = mm3(inverse, work[pl.ds(start, STEP), :], NN)
        work[pl.ds(start, STEP), :] = strip
        s_high, s_low = halves(strip)
        column = lax.broadcasted_iota(jnp.int32, (STEP, n), 1)
        c_high, c_low = halves(jnp.where(column >= start + STEP, strip[:, :n], 0.0))
        lefts[:, :n] = jnp.concatenate([c_high, c_high, c_low, c_low], axis=0)
        rights[:, : 2 * n] = jnp.concatenate([s_high, s_low, s_high, s_low], axis=0)
        for when in service:
            pl.when(p == when)(service[when])
        return carry

    lax.fori_loop(0, n // STEP, panel, 0)


def load_pivot(q, order_row, work):
    n = q.shape[0]
    order_col = jnp.broadcast_to(order_row.astype(F32), (8, n)).T[:, :1]
    column = lax.broadcasted_iota(jnp.int32, (n, n), 1).astype(F32)
    pick = jnp.where(column == order_col, 1.0, 0.0)
    pick16 = pick.astype(B16)
    q_high, q_low = halves(q)
    rows = mm(pick16, q_high, NN) + mm(pick16, q_low, NN)
    r_high, r_low = halves(rows)
    work[:, :n] = mm(r_high, pick16, NT) + mm(r_low, pick16, NT)
    work[:, n:] = pick


def pack(full, ref):
    row = lax.broadcasted_iota(jnp.int32, (HALF, HALF), 0)
    col = lax.broadcasted_iota(jnp.int32, (HALF, HALF), 1)
    last = full[HALF:, HALF:]
    ref[:HALF] = jnp.where(row >= col, full[:HALF, :HALF], last)
    ref[HALF : 2 * HALF] = full[HALF:, :HALF]
    diagonal = jnp.sum(jnp.where(row == col, last, 0.0), axis=0, keepdims=True)
    ref[2 * HALF :] = jnp.broadcast_to(diagonal, (8, HALF))


def unpack(packed):
    row = lax.broadcasted_iota(jnp.int32, (HALF, HALF), 0)
    col = lax.broadcasted_iota(jnp.int32, (HALF, HALF), 1)
    mixed, side, diagonal = packed[:HALF], packed[HALF : 2 * HALF], packed[2 * HALF : 2 * HALF + 1]
    turned = mixed.T
    first = jnp.where(row >= col, mixed, turned)
    last = jnp.where(row < col, mixed, jnp.where(row == col, diagonal, turned))
    return jnp.concatenate(
        [jnp.concatenate([first, side.T], axis=1), jnp.concatenate([side, last], axis=1)], axis=0
    )


def new_targets(slots, left_side, upper_side):
    edge_index = slots // SEP
    west_pos = jnp.where(left_side, 1, 0).astype(jnp.int32)
    north_pos = jnp.where(upper_side, 2, 3).astype(jnp.int32)
    new_edge = jnp.where(
        edge_index == 0,
        west_pos,
        jnp.where(
            edge_index == 1, 1 - west_pos, jnp.where(edge_index == 2, north_pos, 5 - north_pos)
        ),
    )
    return new_edge * SEP + slots % SEP


PACKED = 2 * HALF + 8
Y_NAMES = (
    "shared", "couple_in", "couple_out", "corner_sum", "in0_pass", "in1_pass", "in2_pass", "in3_pass",
    "raw_top_pass", "side0", "side1", "side2", "side3", "low0_pass", "low1_pass",
    "out0_pass", "out1_pass", "out2_pass", "out3_pass", "out4_pass",
)
Z_NAMES = (
    "raw_top", "corner", "in0", "in1", "in2", "in3", "low0", "low1",
    "out0", "out1", "out2", "out3", "out4",
)
NAMES = Y_NAMES + Z_NAMES
Y_COUNT = len(Y_NAMES)
OUTER = ((0, 128), (128, 128), (256, 128), (384, 64), (448, 64))
AFTER_IN = ('low1', 'side0', 'side1', 'side2', 'side3')
PLAN = {0: ((), ('out0',)), 2: (('low0',), ('low0_pass', 'out1')), 4: (('low1',), ('low1_pass', 'out2')), 6: (('out0',), ('out0_pass', 'out3', 'out4'))}
PLAN_A = (('out1',), ('out1_pass',))
PLAN_B = ((), ())


def kernel(
    schur, table,
    first_factor, first_panel, second_factor, second_panel, near, own_high, own_low, far_high, far_low,
    block, a_high, a_low, picks, g_high, g_low,
    shared, shared_o, corner, corner_f, corner_s, corner_o,
    couple, couple_o, raw, raw_o, raw_f, raw_fo,
    panel, panel_o, inner_f, inner_fo, outer_f, outer_fo,
    sides, pivot, work_one, work_two, maps, flag, lefts, rights,
    load_sem, send_sem, recv_sem,
):
    rows = lax.axis_size("gx")
    cols = lax.axis_size("gy")
    pair_rows, pair_cols = rows // 2, cols // 2
    r, c = lax.axis_index("gx"), lax.axis_index("gy")
    row_high, col_high = r // pair_rows, c // pair_cols
    upper, left = r < pair_rows, c < pair_cols
    pair_row, pair_col = r % pair_rows, c % pair_cols
    row_peer = (lax.rem(r + pair_rows, rows), c)
    col_peer = (r, lax.rem(c + pair_cols, cols))

    barrier = pltpu.get_barrier_semaphore()
    for peer in (row_peer, col_peer):
        pl.semaphore_signal(barrier, inc=1, device_id=peer, device_id_type=MESH)

    def part(ref, start, size):
        return ref.at[pl.ds(start, size)]

    ends = {
        "shared": (shared, shared_o),
        "couple_in": (part(couple, 0, 256), part(couple_o, 0, 256)),
        "couple_out": (part(couple, 256, 512), part(couple_o, 256, 512)),
        "corner_sum": (corner_s, corner_o),
        "raw_top_pass": (part(raw_f, 0, 256), part(raw_fo, 0, 256)),
        "raw_top": (part(raw, 0, 256), part(raw_f, 0, 256)),
        "corner": (corner, corner_f),
    }
    for i in range(2):
        ends[f"low{i}_pass"] = (part(raw_f, 256 + 128 * i, 128), part(raw_fo, 256 + 128 * i, 128))
        ends[f"low{i}"] = (part(raw, 256 + 128 * i, 128), part(raw_f, 256 + 128 * i, 128))
    for i in range(4):
        ends[f"in{i}_pass"] = (part(inner_f, 64 * i, 64), part(inner_fo, 64 * i, 64))
        ends[f"in{i}"] = (part(panel, 64 * i, 64), part(inner_f, 64 * i, 64))
        ends[f"side{i}"] = (part(raw, 128 * i, 128), part(raw_o, 128 * i, 128))
    for i, (start, size) in enumerate(OUTER):
        ends[f"out{i}_pass"] = (part(outer_f, start, size), part(outer_fo, start, size))
        ends[f"out{i}"] = (part(panel, 256 + start, size), part(outer_f, start, size))

    def move(name):
        k = NAMES.index(name)
        return pltpu.make_async_remote_copy(
            src_ref=ends[name][0],
            dst_ref=ends[name][1],
            send_sem=send_sem.at[k],
            recv_sem=recv_sem.at[k],
            device_id=row_peer if k < Y_COUNT else col_peer,
            device_id_type=MESH,
        )

    def fence():
        def mark(i, carry):
            flag[...] = jnp.zeros_like(flag)
            return carry

        lax.fori_loop(0, jnp.minimum(r, 0), mark, 0)

    def send(*names):
        for name in names:
            move(name).start()
        fence()

    def arrived(*names):
        for name in names:
            move(name).wait_recv()

    loads = [
        pltpu.make_async_copy(part(schur, 256 * i, 256), part(block, 256 * i, 256), load_sem.at[i])
        for i in range(4)
    ]
    for load in loads:
        load.start()
    fence()

    def listed(first, count, stride=1):
        return jnp.concatenate(
            [table[pl.ds(first + stride * i, 1), :] for i in range(count)], axis=1
        )

    target = new_targets(listed(0, 8), left, upper)
    for i, s in enumerate((0, 3, 1, 2)):
        rank = lax.broadcasted_iota(jnp.int32, (SEP, 4 * SEP), 0) + s * SEP
        picks[i * SEP : (i + 1) * SEP, :] = jnp.where(rank == target, 1.0, 0.0).astype(B16)
    spots = {0: 0, 3: SEP, 1: 2 * SEP, 2: 3 * SEP}

    def gather(start, stop, first):
        chosen = picks[spots[first] : spots[first] + 2 * SEP]
        g_high[start:stop] = mm(a_high[start:stop], chosen, NT).astype(B16)
        g_low[start:stop] = mm(a_low[start:stop], chosen, NT).astype(B16)

    for i in range(4):
        loads[i].wait()
        spot = slice(i * SEP, (i + 1) * SEP)
        a_high[spot], a_low[spot] = halves(block[spot])
        gather(i * SEP, (i + 1) * SEP, 0)

    def picked(s, count, first, width=SEP):
        chosen = picks[spots[s] : spots[s] + count * SEP]
        return mm(chosen, g_high[:, first : first + width], NN) + mm(
            chosen, g_low[:, first : first + width], NN
        )

    raw[:SEP] = picked(1, 1, 0)
    pack(picked(3, 1, SEP), shared)
    pl.semaphore_wait(barrier, 2)
    send("shared", "raw_top")
    pack(picked(0, 1, 0), corner)
    couple[:SEP] = picked(0, 1, SEP)
    send("corner", "couple_in")
    couple[SEP:] = picked(1, 2, SEP)
    send("couple_out")
    raw[SEP:] = picked(2, 1, 0)

    arrived("shared")
    load_pivot(unpack(shared[...] + shared_o[...]), listed(8 + 2 * pair_row, 2), work_one)
    factor_panels(work_one, lefts, rights, SEP, {})
    inverse = halves(work_one[:, SEP:])

    def panel_of(coupling):
        return mm(left_parts(halves(coupling)), right_parts(inverse), NT)

    panel[:SEP] = panel_of(couple[:SEP])
    send("in0", "in1", "in2", "in3")
    panel[SEP:] = panel_of(couple[SEP:])
    arrived("couple_in")
    panel_o[:SEP] = panel_of(couple_o[:SEP])
    mine = pl.ds(pl.multiple_of(row_high * SEP, SEP), SEP)
    theirs = pl.ds(pl.multiple_of((1 - row_high) * SEP, SEP), SEP)
    sides[mine, :SEP] = panel[:SEP]
    sides[theirs, :SEP] = panel_o[:SEP]

    def gram(x):
        pair = halves(x)
        return mm(left_parts(pair), right_parts(pair), NT)

    pivot[...] = -gram(sides[:, :SEP])
    arrived("corner")
    corner_s[...] = corner[...] + corner_f[...]
    send("corner_sum")
    upper_rows = work_one[:, pl.ds(pl.multiple_of(row_high * HALF, HALF), HALF)]
    row = lax.broadcasted_iota(jnp.int32, (SEP, HALF), 0)
    col = lax.broadcasted_iota(jnp.int32, (SEP, HALF), 1) + row_high * HALF
    first_factor[...] = jnp.where(row <= col, upper_rows, 0.0).T
    first_panel[...] = panel[...]
    gather(0, 4 * SEP, 1)
    near[:, : 2 * SEP] = picked(1, 2, 0, 2 * SEP)
    arrived("couple_out")
    panel_o[SEP:] = panel_of(couple_o[SEP:])
    outer = halves(panel[SEP:])
    outer_o = halves(panel_o[SEP:])
    near[:, : 2 * SEP] -= mm(left_parts(outer), right_parts(outer), NT)
    near[:, 2 * SEP :] = -mm(left_parts(outer), right_parts(outer_o), NT)
    arrived("in0")
    send("in0_pass")
    arrived("in1")
    send("in1_pass")
    arrived("in2")
    send("in2_pass")
    arrived("in3")
    send("in3_pass", "low0")
    arrived("raw_top")
    send("raw_top_pass")
    sides[mine, SEP:] = inner_f[...]
    arrived("corner_sum")
    pivot[mine, mine] += unpack(corner_s[...])
    pivot[theirs, theirs] += unpack(corner_o[...])
    arrived("in0_pass", "in1_pass", "in2_pass", "in3_pass")
    send(*AFTER_IN)
    sides[theirs, SEP:] = inner_fo[...]
    n = 2 * SEP
    order = listed(8 + 2 * pair_rows + 4 * pair_row * pair_cols + pair_col, 4, pair_cols)
    load_pivot(pivot[...] - gram(sides[:, SEP:]), order, work_two)

    def step(got, sent):
        def run():
            arrived(*got)
            if sent:
                send(*sent)

        return run

    factor_panels(work_two, lefts, rights, n, {when: step(*lists) for when, lists in PLAN.items()})
    inverse_two = halves(work_two[:, n:])
    s_high, s_low = halves(sides[...])
    maps[...] = -mm(
        left_parts(inverse_two), jnp.concatenate([s_high, s_low, s_high], axis=0), NN
    )
    step(*PLAN_A)()
    mine_two = pl.ds(pl.multiple_of(n + row_high * SEP, SEP), SEP)
    theirs_two = pl.ds(pl.multiple_of(n + (1 - row_high) * SEP, SEP), SEP)
    own_maps = right_parts(halves(work_two[:, mine_two]), halves(maps[:, :SEP]))
    second = mm(left_parts(halves(raw[...]), halves(panel[SEP:])), own_maps, NT)
    second_panel[...] = second
    own_high[...], own_low[...] = halves(second)
    own = (own_high[...], own_low[...])
    near[:, :n] -= mm(left_parts(own), right_parts(own), NT)
    step(*PLAN_B)()
    arrived("side0", "side1", "side2", "side3")
    other_maps = right_parts(halves(work_two[:, theirs_two]), halves(maps[:, :SEP]))
    outer_o = halves(panel_o[SEP:])
    second_o = halves(mm(left_parts(halves(raw_o[...]), outer_o), other_maps, NT))
    near[:, n:] -= mm(left_parts(own), right_parts(second_o), NT)

    lower_rows = work_two[
        pl.ds(pl.multiple_of(col_high * SEP, SEP), SEP), pl.ds(pl.multiple_of(row_high * SEP, SEP), SEP)
    ]
    row = lax.broadcasted_iota(jnp.int32, (SEP, SEP), 0) + col_high * SEP
    col = lax.broadcasted_iota(jnp.int32, (SEP, SEP), 1) + row_high * SEP
    second_factor[...] = jnp.where(row <= col, lower_rows, 0.0).T

    far_maps = right_parts(halves(work_two[:, mine_two]), halves(maps[:, SEP:]))
    far_other_maps = right_parts(halves(work_two[:, theirs_two]), halves(maps[:, SEP:]))

    def far(start, size, raw_ref, outer_ref, map_parts, base):
        spot = slice(start, start + size)
        place = slice(base + start, base + start + size)
        rows_far = mm(left_parts(halves(raw_ref[spot]), halves(outer_ref[spot])), map_parts, NT)
        far_high[place], far_low[place] = halves(rows_far)

    far(0, SEP, raw_f, outer_f, far_maps, 0)
    arrived("out2")
    send("out2_pass")
    arrived("raw_top_pass", "out0_pass", "out1_pass")
    far(0, SEP, raw_fo, outer_fo, far_other_maps, n)
    far(SEP, HALF, raw_f, outer_f, far_maps, 0)
    arrived("out3")
    send("out3_pass")
    arrived("out4")
    send("out4_pass")
    far(SEP + HALF, HALF, raw_f, outer_f, far_maps, 0)
    arrived("low0_pass", "low1_pass", "out2_pass")
    far(SEP, HALF, raw_fo, outer_fo, far_other_maps, n)
    arrived("out3_pass", "out4_pass")
    far(SEP + HALF, HALF, raw_fo, outer_fo, far_other_maps, n)
    for name in NAMES:
        move(name).wait_send()


def finish(
    first_factor, first_panel, second_factor, second_panel, near, own_high, own_low, far_high, far_low,
    out_ff, out_fp, out_sf, out_sp, out_merged, piece, sems,
):
    pair_rows, pair_cols = lax.axis_size("gx") // 2, lax.axis_size("gy") // 2
    row_high, col_high = lax.axis_index("gx") // pair_rows, lax.axis_index("gy") // pair_cols
    n = 2 * SEP

    def columns(number):
        return out_merged.at[:, pl.ds(pl.multiple_of(number * n, n), n)]

    own_slot = 2 * col_high + row_high
    other_slot = 2 * col_high + 1 - row_high
    far_slots = (2 * (1 - col_high) + row_high, 2 * (1 - col_high) + 1 - row_high)
    copies = [
        (near.at[:, :n], columns(own_slot)),
        (near.at[:, n:], columns(other_slot)),
        (second_panel, out_sp),
        (first_panel, out_fp),
        (first_factor, out_ff),
        (second_factor, out_sf),
    ]
    copies = [pltpu.make_async_copy(src, dst, sems.at[i]) for i, (src, dst) in enumerate(copies)]
    for copy in copies:
        copy.start()
    own = left_parts((own_high[...], own_low[...]))
    for i in range(2):
        spot = slice(i * n, (i + 1) * n)
        piece[i] = -mm(own, right_parts((far_high[spot], far_low[spot])), NT)
        copy = pltpu.make_async_copy(piece.at[i], columns(far_slots[i]), sems.at[len(copies)])
        copy.start()
        copies.append(copy)
    for copy in copies:
        copy.wait()


VM = pl.BlockSpec(memory_space=pltpu.VMEM)


def out(*dims):
    return jax.ShapeDtypeStruct(dims, F32)


def out16(*dims):
    return jax.ShapeDtypeStruct(dims, B16)


ANY = pl.BlockSpec(memory_space=pltpu.HBM)


def body(local_schur, boundary_map, order_first, order_second):
    def f32(*dims):
        return pltpu.VMEM(dims, F32)

    def b16(*dims):
        return pltpu.VMEM(dims, B16)

    order_second = order_second.reshape(order_second.shape[:2] + (4, HALF)).transpose(0, 2, 1, 3)
    table = jnp.concatenate(
        [lines.reshape(-1, HALF) for lines in (boundary_map, order_first, order_second)], axis=0
    )
    count = len(NAMES)
    factors = (
        out(SEP // 2, SEP), out(3 * SEP, SEP), out(SEP, SEP), out(2 * SEP, 2 * SEP)
    )
    results = pl.pallas_call(
        kernel,
        out_shape=factors + (
            out(2 * SEP, 4 * SEP), out16(512, 512), out16(512, 512), out16(1024, 512), out16(1024, 512)
        ),
        in_specs=[ANY, VM],
        out_specs=(VM,) * 9,
        scratch_shapes=[
            f32(1024, 1024), b16(1024, 1024), b16(1024, 1024), b16(1024, 1024), b16(1024, 512), b16(1024, 512),
            f32(PACKED, HALF), f32(PACKED, HALF), f32(PACKED, HALF), f32(PACKED, HALF), f32(PACKED, HALF), f32(PACKED, HALF),
            f32(768, 256), f32(768, 256), f32(512, 256), f32(512, 256), f32(512, 256), f32(512, 256),
            f32(768, 256), f32(768, 256), f32(256, 256), f32(256, 256), f32(512, 256), f32(512, 256),
            f32(512, 512), f32(512, 512), f32(256, 512), f32(512, 1024), f32(512, 512), f32(8, 128), b16(256, 512), b16(256, 1024),
            pltpu.SemaphoreType.DMA((4,)), pltpu.SemaphoreType.DMA((count,)), pltpu.SemaphoreType.DMA((count,)),
        ],
        compiler_params=pltpu.CompilerParams(
            collective_id=0, has_side_effects=True, vmem_limit_bytes=44 << 20
        ),
        cost_estimate=pl.CostEstimate(
            flops=20_000_000_000, bytes_accessed=12 << 20, transcendentals=0
        ),
    )(local_schur, table)
    return pl.pallas_call(
        finish,
        out_shape=factors + (out(2 * SEP, 8 * SEP),),
        in_specs=[VM] * 9,
        out_specs=(ANY,) * 5,
        scratch_shapes=[f32(2, 512, 512), pltpu.SemaphoreType.DMA((8,))],
        compiler_params=pltpu.CompilerParams(vmem_limit_bytes=16 << 20),
        cost_estimate=pl.CostEstimate(
            flops=2_000_000_000, bytes_accessed=12 << 20, transcendentals=0
        ),
    )(*results)


def solution(mesh):
    in_specs = (P("gx", "gy"), P("gx", "gy", None), P(None, "gy", None), P())
    out_specs = (P("gx", "gy"),) * 5
    return jax.shard_map(body, mesh=mesh, in_specs=in_specs, out_specs=out_specs, check_vma=False)
```

```python
import jax
import jax.numpy as jnp
from jax import lax
from jax.experimental import pallas as pl
from jax.experimental.pallas import tpu as pltpu
from jax.sharding import PartitionSpec as P

SEP = 256
STEP = 64
HALF = 128
MESH = pl.DeviceIdType.MESH
NN = ((1,), (0,))
NT = ((1,), (1,))
TN = ((0,), (0,))
F32 = jnp.float32
B16 = jnp.bfloat16


def halves(x):
    high = x.astype(B16)
    low = (x - high.astype(F32)).astype(B16)
    return high, low


def mm(a, b, dims):
    return lax.dot_general(a, b, (dims, ((), ())), preferred_element_type=F32)


def mm3(a, b, dims):
    a_high, a_low = halves(a)
    b_high, b_low = halves(b)
    return mm(a_high, b_high, dims) + (mm(a_high, b_low, dims) + mm(a_low, b_high, dims))


def left_parts(*pairs):
    return jnp.concatenate([part for high, low in pairs for part in (high, high, low)], axis=1)


def right_parts(*pairs):
    return jnp.concatenate([part for high, low in pairs for part in (high, low, high)], axis=1)


def eliminate(tiles):
    count = len(tiles)
    sub = lax.broadcasted_iota(jnp.int32, (8, 128), 0)
    for t in range(count):
        cols = {
            g: [jnp.broadcast_to(tiles[g][:, 8 * t + k : 8 * t + k + 1], (8, 128)) for k in range(8)]
            for g in range(t, count)
        }
        for k in range(8):
            scale = lax.rsqrt(cols[t][k][k : k + 1, :])
            final_row = tiles[t][k : k + 1, :] * scale
            diag_row = [cols[t][m][k : k + 1, :] * scale for m in range(k + 1, 8)]
            for g in range(t, count):
                factor = cols[g][k] * scale
                if g == t:
                    factor = jnp.where(sub > k, factor, 0.0)
                for m in range(k + 1, 8):
                    cols[g][m] = cols[g][m] - factor * diag_row[m - k - 1]
                tiles[g] = tiles[g] - factor * final_row
            tiles[t] = jnp.where(sub == k, final_row, tiles[t])
    return tiles


def factor_panels(work, lefts, rights, n, service):
    lane = lax.broadcasted_iota(jnp.int32, (STEP, 128), 1)
    eye = jnp.where(lane == lax.broadcasted_iota(jnp.int32, (STEP, 128), 0) + STEP, 1.0, 0.0)
    lefts[:, :n] = jnp.zeros((4 * STEP, n), B16)
    rights[:, : 2 * n] = jnp.zeros((4 * STEP, 2 * n), B16)

    def panel(p, carry):
        start = pl.multiple_of(p * STEP, STEP)
        base = pl.multiple_of((p // 2) * 128, 128)
        even = p % 2 == 0
        near_delta = mm(lefts[:, pl.ds(base, 128)], rights[:, pl.ds(base, 128)], TN)
        block = work[pl.ds(start, STEP), pl.ds(base, 128)]
        block = block - jnp.where(even, near_delta[:STEP], near_delta[STEP:])
        block = jnp.where(even, block, pltpu.roll(block, STEP, 1))
        block = jnp.where(lane < STEP, block, eye)
        work[...] -= mm(lefts[:, :n], rights[:, : 2 * n], TN)
        tiles = eliminate([block[8 * g : 8 * g + 8, :] for g in range(STEP // 8)])
        inverse = jnp.concatenate(tiles, axis=0)[:, STEP:]
        strip = mm3(inverse, work[pl.ds(start, STEP), :], NN)
        work[pl.ds(start, STEP), :] = strip
        s_high, s_low = halves(strip)
        column = lax.broadcasted_iota(jnp.int32, (STEP, n), 1)
        c_high, c_low = halves(jnp.where(column >= start + STEP, strip[:, :n], 0.0))
        lefts[:, :n] = jnp.concatenate([c_high, c_high, c_low, c_low], axis=0)
        rights[:, : 2 * n] = jnp.concatenate([s_high, s_low, s_high, s_low], axis=0)
        for when in service:
            pl.when(p == when)(service[when])
        return carry

    lax.fori_loop(0, n // STEP, panel, 0)


def load_pivot(q, order_row, work):
    n = q.shape[0]
    order_col = jnp.broadcast_to(order_row.astype(F32), (8, n)).T[:, :1]
    column = lax.broadcasted_iota(jnp.int32, (n, n), 1).astype(F32)
    pick = jnp.where(column == order_col, 1.0, 0.0)
    pick16 = pick.astype(B16)
    q_high, q_low = halves(q)
    rows = mm(pick16, q_high, NN) + mm(pick16, q_low, NN)
    r_high, r_low = halves(rows)
    work[:, :n] = mm(r_high, pick16, NT) + mm(r_low, pick16, NT)
    work[:, n:] = pick


def pack(full, ref):
    row = lax.broadcasted_iota(jnp.int32, (HALF, HALF), 0)
    col = lax.broadcasted_iota(jnp.int32, (HALF, HALF), 1)
    last = full[HALF:, HALF:]
    ref[:HALF] = jnp.where(row >= col, full[:HALF, :HALF], last)
    ref[HALF : 2 * HALF] = full[HALF:, :HALF]
    diagonal = jnp.sum(jnp.where(row == col, last, 0.0), axis=0, keepdims=True)
    ref[2 * HALF :] = jnp.broadcast_to(diagonal, (8, HALF))


def unpack(packed):
    row = lax.broadcasted_iota(jnp.int32, (HALF, HALF), 0)
    col = lax.broadcasted_iota(jnp.int32, (HALF, HALF), 1)
    mixed, side, diagonal = packed[:HALF], packed[HALF : 2 * HALF], packed[2 * HALF : 2 * HALF + 1]
    turned = mixed.T
    first = jnp.where(row >= col, mixed, turned)
    last = jnp.where(row < col, mixed, jnp.where(row == col, diagonal, turned))
    return jnp.concatenate(
        [jnp.concatenate([first, side.T], axis=1), jnp.concatenate([side, last], axis=1)], axis=0
    )


def new_targets(slots, left_side, upper_side):
    edge_index = slots // SEP
    west_pos = jnp.where(left_side, 1, 0).astype(jnp.int32)
    north_pos = jnp.where(upper_side, 2, 3).astype(jnp.int32)
    new_edge = jnp.where(
        edge_index == 0,
        west_pos,
        jnp.where(
            edge_index == 1, 1 - west_pos, jnp.where(edge_index == 2, north_pos, 5 - north_pos)
        ),
    )
    return new_edge * SEP + slots % SEP


PACKED = 2 * HALF + 8
Y_NAMES = (
    "shared", "couple_in", "couple_out", "corner_sum", "in0_pass", "in1_pass", "in2_pass", "in3_pass",
    "raw_top_pass", "side0", "side1", "side2", "side3", "low0_pass", "low1_pass",
    "out0_pass", "out1_pass", "out2_pass", "out3_pass", "out4_pass",
)
Z_NAMES = (
    "raw_top", "corner", "in0", "in1", "in2", "in3", "low0", "low1",
    "out0", "out1", "out2", "out3", "out4",
)
NAMES = Y_NAMES + Z_NAMES
Y_COUNT = len(Y_NAMES)
OUTER = ((0, 128), (128, 128), (256, 128), (384, 64), (448, 64))
AFTER_IN = ('low1', 'side0', 'side1', 'side2', 'side3')
PLAN = {0: ((), ('out0',)), 2: (('low0',), ('low0_pass', 'out1')), 4: (('low1',), ('low1_pass', 'out2')), 6: (('out0',), ('out0_pass', 'out3', 'out4'))}
PLAN_A = (('out1',), ('out1_pass',))
PLAN_B = ((), ())


def kernel(
    schur, table,
    first_factor, first_panel, second_factor, second_panel, near, own_high, own_low, far_high, far_low,
    block, a_high, a_low, picks, g_high, g_low,
    shared, shared_o, corner, corner_f, corner_s, corner_o,
    couple, couple_o, raw, raw_o, raw_f, raw_fo,
    panel, panel_o, inner_f, inner_fo, outer_f, outer_fo,
    sides, pivot, work_one, work_two, maps, flag, lefts, rights,
    load_sem, send_sem, recv_sem,
):
    rows = lax.axis_size("gx")
    cols = lax.axis_size("gy")
    pair_rows, pair_cols = rows // 2, cols // 2
    r, c = lax.axis_index("gx"), lax.axis_index("gy")
    row_high, col_high = r // pair_rows, c // pair_cols
    upper, left = r < pair_rows, c < pair_cols
    pair_row, pair_col = r % pair_rows, c % pair_cols
    row_peer = (lax.rem(r + pair_rows, rows), c)
    col_peer = (r, lax.rem(c + pair_cols, cols))

    barrier = pltpu.get_barrier_semaphore()
    for peer in (row_peer, col_peer):
        pl.semaphore_signal(barrier, inc=1, device_id=peer, device_id_type=MESH)

    def part(ref, start, size):
        return ref.at[pl.ds(start, size)]

    ends = {
        "shared": (shared, shared_o),
        "couple_in": (part(couple, 0, 256), part(couple_o, 0, 256)),
        "couple_out": (part(couple, 256, 512), part(couple_o, 256, 512)),
        "corner_sum": (corner_s, corner_o),
        "raw_top_pass": (part(raw_f, 0, 256), part(raw_fo, 0, 256)),
        "raw_top": (part(raw, 0, 256), part(raw_f, 0, 256)),
        "corner": (corner, corner_f),
    }
    for i in range(2):
        ends[f"low{i}_pass"] = (part(raw_f, 256 + 128 * i, 128), part(raw_fo, 256 + 128 * i, 128))
        ends[f"low{i}"] = (part(raw, 256 + 128 * i, 128), part(raw_f, 256 + 128 * i, 128))
    for i in range(4):
        ends[f"in{i}_pass"] = (part(inner_f, 64 * i, 64), part(inner_fo, 64 * i, 64))
        ends[f"in{i}"] = (part(panel, 64 * i, 64), part(inner_f, 64 * i, 64))
        ends[f"side{i}"] = (part(raw, 128 * i, 128), part(raw_o, 128 * i, 128))
    for i, (start, size) in enumerate(OUTER):
        ends[f"out{i}_pass"] = (part(outer_f, start, size), part(outer_fo, start, size))
        ends[f"out{i}"] = (part(panel, 256 + start, size), part(outer_f, start, size))

    def move(name):
        k = NAMES.index(name)
        return pltpu.make_async_remote_copy(
            src_ref=ends[name][0],
            dst_ref=ends[name][1],
            send_sem=send_sem.at[k],
            recv_sem=recv_sem.at[k],
            device_id=row_peer if k < Y_COUNT else col_peer,
            device_id_type=MESH,
        )

    def fence():
        def mark(i, carry):
            flag[...] = jnp.zeros_like(flag)
            return carry

        lax.fori_loop(0, jnp.minimum(r, 0), mark, 0)

    def send(*names):
        for name in names:
            move(name).start()
        fence()

    def arrived(*names):
        for name in names:
            move(name).wait_recv()

    loads = [
        pltpu.make_async_copy(part(schur, 256 * i, 256), part(block, 256 * i, 256), load_sem.at[i])
        for i in range(4)
    ]
    for load in loads:
        load.start()
    fence()

    def listed(first, count, stride=1):
        return jnp.concatenate(
            [table[pl.ds(first + stride * i, 1), :] for i in range(count)], axis=1
        )

    target = new_targets(listed(0, 8), left, upper)
    for i, s in enumerate((0, 3, 1, 2)):
        rank = lax.broadcasted_iota(jnp.int32, (SEP, 4 * SEP), 0) + s * SEP
        picks[i * SEP : (i + 1) * SEP, :] = jnp.where(rank == target, 1.0, 0.0).astype(B16)
    spots = {0: 0, 3: SEP, 1: 2 * SEP, 2: 3 * SEP}

    def gather(start, stop, first):
        chosen = picks[spots[first] : spots[first] + 2 * SEP]
        g_high[start:stop] = mm(a_high[start:stop], chosen, NT).astype(B16)
        g_low[start:stop] = mm(a_low[start:stop], chosen, NT).astype(B16)

    for i in range(4):
        loads[i].wait()
        spot = slice(i * SEP, (i + 1) * SEP)
        a_high[spot], a_low[spot] = halves(block[spot])
        gather(i * SEP, (i + 1) * SEP, 0)

    def picked(s, count, first, width=SEP):
        chosen = picks[spots[s] : spots[s] + count * SEP]
        return mm(chosen, g_high[:, first : first + width], NN) + mm(
            chosen, g_low[:, first : first + width], NN
        )

    raw[:SEP] = picked(1, 1, 0)
    pack(picked(3, 1, SEP), shared)
    pl.semaphore_wait(barrier, 2)
    send("shared", "raw_top")
    pack(picked(0, 1, 0), corner)
    couple[:SEP] = picked(0, 1, SEP)
    send("corner", "couple_in")
    couple[SEP:] = picked(1, 2, SEP)
    send("couple_out")
    raw[SEP:] = picked(2, 1, 0)
    gather(0, 4 * SEP, 1)
    near[:, : 2 * SEP] = picked(1, 2, 0, 2 * SEP)

    arrived("shared")
    load_pivot(unpack(shared[...] + shared_o[...]), listed(8 + 2 * pair_row, 2), work_one)
    factor_panels(work_one, lefts, rights, SEP, {})
    inverse = halves(work_one[:, SEP:])

    def panel_of(coupling):
        return mm(left_parts(halves(coupling)), right_parts(inverse), NT)

    panel[:SEP] = panel_of(couple[:SEP])
    send("in0", "in1", "in2", "in3")
    panel[SEP:] = panel_of(couple[SEP:])
    arrived("couple_in")
    panel_o[:SEP] = panel_of(couple_o[:SEP])
    mine = pl.ds(pl.multiple_of(row_high * SEP, SEP), SEP)
    theirs = pl.ds(pl.multiple_of((1 - row_high) * SEP, SEP), SEP)
    sides[mine, :SEP] = panel[:SEP]
    sides[theirs, :SEP] = panel_o[:SEP]

    def gram(x):
        pair = halves(x)
        return mm(left_parts(pair), right_parts(pair), NT)

    pivot[...] = -gram(sides[:, :SEP])
    arrived("corner")
    corner_s[...] = corner[...] + corner_f[...]
    send("corner_sum")
    upper_rows = work_one[:, pl.ds(pl.multiple_of(row_high * HALF, HALF), HALF)]
    row = lax.broadcasted_iota(jnp.int32, (SEP, HALF), 0)
    col = lax.broadcasted_iota(jnp.int32, (SEP, HALF), 1) + row_high * HALF
    first_factor[...] = jnp.where(row <= col, upper_rows, 0.0).T
    first_panel[...] = panel[...]
    arrived("couple_out")
    panel_o[SEP:] = panel_of(couple_o[SEP:])
    outer = halves(panel[SEP:])
    outer_o = halves(panel_o[SEP:])
    near[:, : 2 * SEP] -= mm(left_parts(outer), right_parts(outer), NT)
    near[:, 2 * SEP :] = -mm(left_parts(outer), right_parts(outer_o), NT)
    arrived("in0")
    send("in0_pass")
    arrived("in1")
    send("in1_pass")
    arrived("in2")
    send("in2_pass")
    arrived("in3")
    send("in3_pass", "low0")
    arrived("raw_top")
    send("raw_top_pass")
    sides[mine, SEP:] = inner_f[...]
    arrived("corner_sum")
    pivot[mine, mine] += unpack(corner_s[...])
    pivot[theirs, theirs] += unpack(corner_o[...])
    arrived("in0_pass", "in1_pass", "in2_pass", "in3_pass")
    send(*AFTER_IN)
    sides[theirs, SEP:] = inner_fo[...]
    n = 2 * SEP
    order = listed(8 + 2 * pair_rows + 4 * pair_row * pair_cols + pair_col, 4, pair_cols)
    load_pivot(pivot[...] - gram(sides[:, SEP:]), order, work_two)

    def step(got, sent):
        def run():
            arrived(*got)
            if sent:
                send(*sent)

        return run

    factor_panels(work_two, lefts, rights, n, {when: step(*lists) for when, lists in PLAN.items()})
    inverse_two = halves(work_two[:, n:])
    s_high, s_low = halves(sides[...])
    maps[...] = -mm(
        left_parts(inverse_two), jnp.concatenate([s_high, s_low, s_high], axis=0), NN
    )
    step(*PLAN_A)()
    mine_two = pl.ds(pl.multiple_of(n + row_high * SEP, SEP), SEP)
    theirs_two = pl.ds(pl.multiple_of(n + (1 - row_high) * SEP, SEP), SEP)
    own_maps = right_parts(halves(work_two[:, mine_two]), halves(maps[:, :SEP]))
    second = mm(left_parts(halves(raw[...]), halves(panel[SEP:])), own_maps, NT)
    second_panel[...] = second
    own_high[...], own_low[...] = halves(second)
    own = (own_high[...], own_low[...])
    near[:, :n] -= mm(left_parts(own), right_parts(own), NT)
    step(*PLAN_B)()
    arrived("side0", "side1", "side2", "side3")
    other_maps = right_parts(halves(work_two[:, theirs_two]), halves(maps[:, :SEP]))
    outer_o = halves(panel_o[SEP:])
    second_o = halves(mm(left_parts(halves(raw_o[...]), outer_o), other_maps, NT))
    near[:, n:] -= mm(left_parts(own), right_parts(second_o), NT)

    lower_rows = work_two[
        pl.ds(pl.multiple_of(col_high * SEP, SEP), SEP), pl.ds(pl.multiple_of(row_high * SEP, SEP), SEP)
    ]
    row = lax.broadcasted_iota(jnp.int32, (SEP, SEP), 0) + col_high * SEP
    col = lax.broadcasted_iota(jnp.int32, (SEP, SEP), 1) + row_high * SEP
    second_factor[...] = jnp.where(row <= col, lower_rows, 0.0).T

    far_maps = right_parts(halves(work_two[:, mine_two]), halves(maps[:, SEP:]))
    far_other_maps = right_parts(halves(work_two[:, theirs_two]), halves(maps[:, SEP:]))

    def far(start, size, raw_ref, outer_ref, map_parts, base):
        spot = slice(start, start + size)
        place = slice(base + start, base + start + size)
        rows_far = mm(left_parts(halves(raw_ref[spot]), halves(outer_ref[spot])), map_parts, NT)
        far_high[place], far_low[place] = halves(rows_far)

    far(0, SEP, raw_f, outer_f, far_maps, 0)
    arrived("out2")
    send("out2_pass")
    arrived("raw_top_pass", "out0_pass", "out1_pass")
    far(0, SEP, raw_fo, outer_fo, far_other_maps, n)
    far(SEP, HALF, raw_f, outer_f, far_maps, 0)
    arrived("out3")
    send("out3_pass")
    arrived("out4")
    send("out4_pass")
    far(SEP + HALF, HALF, raw_f, outer_f, far_maps, 0)
    arrived("low0_pass", "low1_pass", "out2_pass")
    far(SEP, HALF, raw_fo, outer_fo, far_other_maps, n)
    arrived("out3_pass", "out4_pass")
    far(SEP + HALF, HALF, raw_fo, outer_fo, far_other_maps, n)
    for name in NAMES:
        move(name).wait_send()


def finish(
    first_factor, first_panel, second_factor, second_panel, near, own_high, own_low, far_high, far_low,
    out_ff, out_fp, out_sf, out_sp, out_merged, piece, sems,
):
    pair_rows, pair_cols = lax.axis_size("gx") // 2, lax.axis_size("gy") // 2
    row_high, col_high = lax.axis_index("gx") // pair_rows, lax.axis_index("gy") // pair_cols
    n = 2 * SEP

    def columns(number):
        return out_merged.at[:, pl.ds(pl.multiple_of(number * n, n), n)]

    own_slot = 2 * col_high + row_high
    other_slot = 2 * col_high + 1 - row_high
    far_slots = (2 * (1 - col_high) + row_high, 2 * (1 - col_high) + 1 - row_high)
    copies = [
        (near.at[:, :n], columns(own_slot)),
        (near.at[:, n:], columns(other_slot)),
        (second_panel, out_sp),
        (first_panel, out_fp),
        (first_factor, out_ff),
        (second_factor, out_sf),
    ]
    copies = [pltpu.make_async_copy(src, dst, sems.at[i]) for i, (src, dst) in enumerate(copies)]
    for copy in copies:
        copy.start()
    own = left_parts((own_high[...], own_low[...]))
    for i in range(4):
        spot = slice(i * SEP, (i + 1) * SEP)
        piece[i] = -mm(own, right_parts((far_high[spot], far_low[spot])), NT)
        start = pl.multiple_of(far_slots[i // 2] * n + i % 2 * SEP, SEP)
        copy = pltpu.make_async_copy(
            piece.at[i], out_merged.at[:, pl.ds(start, SEP)], sems.at[len(copies)]
        )
        copy.start()
        copies.append(copy)
    for copy in copies:
        copy.wait()


VM = pl.BlockSpec(memory_space=pltpu.VMEM)


def out(*dims):
    return jax.ShapeDtypeStruct(dims, F32)


def out16(*dims):
    return jax.ShapeDtypeStruct(dims, B16)


ANY = pl.BlockSpec(memory_space=pltpu.HBM)


def body(local_schur, boundary_map, order_first, order_second):
    def f32(*dims):
        return pltpu.VMEM(dims, F32)

    def b16(*dims):
        return pltpu.VMEM(dims, B16)

    order_second = order_second.reshape(order_second.shape[:2] + (4, HALF)).transpose(0, 2, 1, 3)
    table = jnp.concatenate(
        [lines.reshape(-1, HALF) for lines in (boundary_map, order_first, order_second)], axis=0
    )
    count = len(NAMES)
    factors = (
        out(SEP // 2, SEP), out(3 * SEP, SEP), out(SEP, SEP), out(2 * SEP, 2 * SEP)
    )
    results = pl.pallas_call(
        kernel,
        out_shape=factors + (
            out(2 * SEP, 4 * SEP), out16(512, 512), out16(512, 512), out16(1024, 512), out16(1024, 512)
        ),
        in_specs=[ANY, VM],
        out_specs=(VM,) * 9,
        scratch_shapes=[
            f32(1024, 1024), b16(1024, 1024), b16(1024, 1024), b16(1024, 1024), b16(1024, 512), b16(1024, 512),
            f32(PACKED, HALF), f32(PACKED, HALF), f32(PACKED, HALF), f32(PACKED, HALF), f32(PACKED, HALF), f32(PACKED, HALF),
            f32(768, 256), f32(768, 256), f32(512, 256), f32(512, 256), f32(512, 256), f32(512, 256),
            f32(768, 256), f32(768, 256), f32(256, 256), f32(256, 256), f32(512, 256), f32(512, 256),
            f32(512, 512), f32(512, 512), f32(256, 512), f32(512, 1024), f32(512, 512), f32(8, 128), b16(256, 512), b16(256, 1024),
            pltpu.SemaphoreType.DMA((4,)), pltpu.SemaphoreType.DMA((count,)), pltpu.SemaphoreType.DMA((count,)),
        ],
        compiler_params=pltpu.CompilerParams(
            collective_id=0, has_side_effects=True, vmem_limit_bytes=44 << 20
        ),
        cost_estimate=pl.CostEstimate(
            flops=20_000_000_000, bytes_accessed=12 << 20, transcendentals=0
        ),
    )(local_schur, table)
    return pl.pallas_call(
        finish,
        out_shape=factors + (out(2 * SEP, 8 * SEP),),
        in_specs=[VM] * 9,
        out_specs=(ANY,) * 5,
        scratch_shapes=[f32(4, 512, 256), pltpu.SemaphoreType.DMA((10,))],
        compiler_params=pltpu.CompilerParams(vmem_limit_bytes=16 << 20),
        cost_estimate=pl.CostEstimate(
            flops=2_000_000_000, bytes_accessed=12 << 20, transcendentals=0
        ),
    )(*results)


def solution(mesh):
    in_specs = (P("gx", "gy"), P("gx", "gy", None), P(None, "gy", None), P())
    out_specs = (P("gx", "gy"),) * 5
    return jax.shard_map(body, mesh=mesh, in_specs=in_specs, out_specs=out_specs, check_vma=False)
```
